32 devices in a mesh: group: 2 (over x), blk: 8 (over z, y), ulysses: 2 (over core).
Axes of the slice: x: 2, y: 2, z: 4, core: 2. Of those that a mesh axis runs over, the one named last changes fastest.
Arguments:
- query_int: bfloat16 [4096, 8192], P(('group', 'blk', 'ulysses')), parts along dimension 0, may hold values from -127 to 127, as said below
- key_int: bfloat16 [4096, 1024], P(('group', 'blk', 'ulysses')), parts along dimension 0, may hold values from -127 to 127, as said below
- values: bfloat16 [4096, 1024], P(('group', 'blk', 'ulysses')), parts along dimension 0, may hold values from -6 to 6
- query_scale: bfloat16 [32, 64], P(('group', 'blk')), parts along dimension 0, may hold values from 0.001 to 0.02
- key_scale: bfloat16 [32, 8], P('group'), parts along dimension 0, may hold values from 0.002 to 0.04
- verticals: int32 [16, 8], P('group'), parts along dimension 0, may hold values from 0 to 15, as said below
- slashes: int32 [16, 8], P('group'), parts along dimension 0, may hold values from 0 to 8, as said below
Outputs:
- attention: bfloat16 [4096, 8192], P(('group', 'blk', 'ulysses')), parts along dimension 0
The draws below stay inside these ranges and needn't reach their ends.
There are 2 independent parts, one for each index of `group`. The reference program is written for one: setup_inputs(seed, part) draws one part's arguments, and reference() takes and returns one part's arrays. A program takes and returns all parts, laid end to end along the dimension named above; each array names one. Nothing has to cross between parts.
Inputs may be any that keep to these rules, and one draw needn't show every extreme that they name: `query_int`: integer values. `key_int`: integer values. `verticals`: each row holds 8 distinct key blocks, block 0 among them. `slashes`: each row holds 8 distinct offsets, 0 among them.
All inputs are finite; a program needn't handle non-finite values.
Results may differ from the reference program's by a relative error of at most 0.0019.
Values may be sent and summed in bfloat16 or wider, within the bound.
A program may use at most 128 MiB of HBM per device.

```python
import jax
import jax.numpy as jnp
from jax import lax

H = 64
KVH = 8
DH = 128
BLOCK = 128
BPD = 2
NV = 8
NSL = 8
SPAN = 4
QB = 16
SEQ = 2048


def integer_pair(key):
    keys_drawn = jax.random.randint(jax.random.fold_in(key, 101), (SEQ, KVH * DH), -127, 128)
    queries_drawn = jax.random.randint(jax.random.fold_in(key, 202), (SEQ, H * DH), -127, 128)
    return (queries_drawn.astype(jnp.float32), keys_drawn.astype(jnp.float32))


def draw_query_int(key, part):
    queries_drawn, keys_drawn = integer_pair(key)
    return queries_drawn.astype(jnp.bfloat16)


def draw_key_int(key, part):
    queries_drawn, keys_drawn = integer_pair(key)
    return keys_drawn.astype(jnp.bfloat16)


def log_between(key, shape, lower, upper):
    return jnp.exp(jax.random.uniform(key, shape, jnp.float32, jnp.log(lower), jnp.log(upper)))


def draw_query_scale(key, part):
    local_key = jax.random.fold_in(key, 303)
    drawn = log_between(local_key, (QB, H), 0.00101, 0.0199)
    return drawn.astype(jnp.bfloat16)


def draw_key_scale(key, part):
    local_key = jax.random.fold_in(key, 404)
    drawn = log_between(local_key, (QB, KVH), 0.00202, 0.0398)
    return drawn.astype(jnp.bfloat16)


def distinct_rows(key, tag, upper, picks):

    def one_row(row_index):
        order = jax.random.permutation(jax.random.fold_in(jax.random.fold_in(key, tag), row_index), upper - 1) + 1
        return jnp.concatenate([jnp.zeros((1,), jnp.int32), order[:picks - 1].astype(jnp.int32)])
    rows_drawn = jax.vmap(one_row)(jnp.arange(KVH))
    return rows_drawn.at[0, picks - 1].set(upper)


def draw_verticals(key, part):
    return distinct_rows(key, 505, QB - 1, NV)


def draw_slashes(key, part):
    return distinct_rows(key, 606, SPAN * BPD, NSL)


def levels(key, shape, shards, low, top_value):
    def one(dim, parts):
        steps = jax.random.uniform(jax.random.fold_in(jax.random.fold_in(key, 6), dim), (parts,), jnp.float32, low / len(shards), top_value / len(shards))
        return jnp.repeat(jnp.exp(steps), shape[dim] // parts).reshape((-1,) + (1,) * (len(shape) - dim - 1))

    level = one(*shards[0])
    for cut in shards[1:]:
        level = level * one(*cut)
    return level


def scatter_about(own_key, shape, scale, limit, cuts=(), kind=jnp.bfloat16):
    loudness = levels(own_key, shape, cuts, -0.22, 0.18) if cuts else 1.0
    values = jax.random.normal(own_key, shape, jnp.float32) * scale * loudness
    return jnp.minimum(jnp.maximum(values, -limit), limit).astype(kind)


def setup_inputs(seed: int = 0, part: int = 0) -> dict:
    arg_keys = jax.random.split(jax.random.key(seed), 8)
    own_keys = jax.random.split(jax.random.fold_in(arg_keys[7], part), 8)
    return {
        "query_int": draw_query_int(jax.random.fold_in(jax.random.fold_in(arg_keys[7], part), 71), part),
        "key_int": draw_key_int(jax.random.fold_in(jax.random.fold_in(arg_keys[7], part), 71), part),
        "values": scatter_about(own_keys[2], (SEQ, KVH * DH), 1.0, 6.0, ((0, 16),)),
        "query_scale": draw_query_scale(jax.random.fold_in(jax.random.fold_in(arg_keys[7], part), 71), part),
        "key_scale": draw_key_scale(jax.random.fold_in(jax.random.fold_in(arg_keys[7], part), 71), part),
        "verticals": draw_verticals(jax.random.fold_in(jax.random.fold_in(arg_keys[7], part), 71), part),
        "slashes": draw_slashes(jax.random.fold_in(jax.random.fold_in(arg_keys[7], part), 71), part),
    }


FLOOR_SCORE = -1e30


def block_table(verticals, slashes, first_block, block_count):
    blocks = first_block + jnp.arange(block_count, dtype=jnp.int32)
    slash_keys = blocks[:, None, None] - slashes[None, :, :]
    slash_live = slash_keys >= 0
    vert_keys = jnp.broadcast_to(verticals[None, :, :], (block_count,) + verticals.shape)
    clashes = jnp.any((vert_keys[:, :, :, None] == slash_keys[:, :, None, :]) & slash_live[:, :, None, :], axis=3)
    vert_live = (vert_keys <= blocks[:, None, None]) & jnp.logical_not(clashes)
    return (jnp.concatenate([vert_keys, slash_keys], axis=2), jnp.concatenate([vert_live, slash_live], axis=2), blocks)


def attend_block(query_block, query_scales, key_blocks, value_blocks, key_scales, live_slots, diagonal):
    dots = jnp.einsum("tgpd,gnsd->gptns", query_block.astype(jnp.float32), key_blocks.astype(jnp.float32))
    scores = dots * query_scales[:, :, None, None, None] * key_scales[:, None, None, :, None]
    width = query_block.shape[0]
    causal = jnp.arange(width)[None, :] <= jnp.arange(width)[:, None]
    allowed = live_slots[:, None, None, :, None] & (jnp.logical_not(diagonal)[:, None, None, :, None] | causal[None, None, :, None, :])
    masked = jnp.where(allowed, scores, FLOOR_SCORE)
    largest = jnp.max(masked, axis=(3, 4), keepdims=True)
    weights = jnp.where(allowed, jnp.exp(masked - largest), 0.0)
    totals = jnp.sum(weights, axis=(3, 4))
    probs = weights.astype(jnp.bfloat16)
    numer = jnp.einsum("gptns,gnsd->tgpd", probs.astype(jnp.float32), value_blocks.astype(jnp.float32))
    return (numer / jnp.transpose(totals, (2, 0, 1))[:, :, :, None]).astype(jnp.bfloat16)


def reference(query_int, key_int, values, query_scale, key_scale, verticals, slashes):
    per_group = H // KVH
    key_shaped = key_int.reshape(QB, BLOCK, KVH, DH)
    value_shaped = values.reshape(QB, BLOCK, KVH, DH)
    group_ids = jnp.arange(KVH, dtype=jnp.int32)

    def one_block(block_index):
        block_keys, live_slots, blocks = block_table(verticals, slashes, block_index, 1)
        clipped = jnp.clip(block_keys[0], 0, QB - 1).astype(jnp.int32)
        key_blocks = key_shaped[clipped, :, group_ids[:, None], :]
        value_blocks = value_shaped[clipped, :, group_ids[:, None], :]
        key_scales = key_scale[clipped, group_ids[:, None]].astype(jnp.float32)
        start_row = (block_index * BLOCK).astype(jnp.int32)
        query_block = lax.dynamic_slice_in_dim(query_int, start_row, BLOCK, 0).reshape(BLOCK, KVH, per_group, DH)
        query_scales = lax.dynamic_slice_in_dim(query_scale, block_index.astype(jnp.int32), 1, 0).astype(jnp.float32).reshape(KVH, per_group)
        diagonal = block_keys[0] == block_index
        return attend_block(query_block, query_scales, key_blocks, value_blocks, key_scales, live_slots[0], diagonal)

    outputs = lax.map(one_block, jnp.arange(QB, dtype=jnp.int32))
    return outputs.reshape(SEQ, H * DH)
```

```python
import functools
import math

import jax
import jax.numpy as jnp
from jax import lax
from jax.experimental import pallas as pl
from jax.experimental.pallas import tpu as pltpu
from jax.sharding import PartitionSpec as P

BLOCK = 128
DH = 128
BIG = 2.0**40
LOG2E = math.log2(math.e)
MESH = pl.DeviceIdType.MESH
UP, ACROSS, CHIP = 0, 1, 2


def kernel(
    rows, heads, groups, blocks, q_hbm, k_hbm, v_hbm, qs_hbm, ks_hbm, vert_hbm, slash_hbm, o_ref,
    q_ref, kv_ref, m_ref, l_ref, acc_ref, qs_ref, ks_ref, vert_ref, slash_ref,
    table_ref, scalar_ref, local_sem, small_sem,
    up_send, across_send, chip_send, up_recv, across_recv, chip_recv, last_recv, chip_last_recv,
):
    span = lax.axis_index("blk")
    core = lax.axis_index("ulysses")
    row, col = span // 2, span % 2
    mine = span * 2 + core
    per_group = heads // groups
    width = per_group * DH
    parts = local_sem.shape[0]
    per_part = groups // parts
    half = groups // 2

    def block_of(r, c, u):
        return (r * 2 + c) * 2 + u

    targets = {
        UP: {"blk": span + 2, "ulysses": core},
        ACROSS: {"blk": row * 2 + 1 - col, "ulysses": core},
        CHIP: {"blk": span, "ulysses": 1 - core},
    }

    def remote(place, way, send_sem, recv_sem):
        return pltpu.make_async_remote_copy(
            src_ref=place,
            dst_ref=place,
            send_sem=send_sem,
            recv_sem=recv_sem,
            device_id=targets[way],
            device_id_type=MESH,
        )

    def piece(part, block):
        return kv_ref.at[pl.ds(part * per_part, per_part), block]

    def one(g, block):
        return kv_ref.at[pl.ds(g, 1), block]

    def up(part, k, block):
        return remote(piece(part, block), UP, up_send.at[k], up_recv.at[part, k])

    def across(part, k, block):
        return remote(piece(part, block), ACROSS, across_send.at[k], across_recv.at[part, k])

    def chip(part, k, block, crossing):
        return remote(
            piece(part, block), CHIP, chip_send.at[crossing, k], chip_recv.at[part, k + crossing]
        )

    def last_across(g, block):
        return remote(one(g, block), ACROSS, across_send.at[row], last_recv.at[g])

    def last_up(g, block):
        return remote(one(g, block), UP, up_send.at[rows], last_recv.at[g])

    def last_chip(g, block):
        return remote(one(g, block), CHIP, chip_send.at[1, row], chip_last_recv.at[g])

    def local_copy(part, which, i):
        g = part * per_part + i
        return pltpu.make_async_copy(
            (k_hbm, v_hbm)[which].at[:, pl.ds(g * DH, DH)],
            kv_ref.at[g, mine, which],
            local_sem.at[part],
        )

    small = [
        pltpu.make_async_copy(src, dst, small_sem.at[i])
        for i, (src, dst) in enumerate(
            [(qs_hbm, qs_ref), (ks_hbm, ks_ref), (vert_hbm, vert_ref), (slash_hbm, slash_ref)]
        )
    ]
    to_scalars = pltpu.make_async_copy(table_ref, scalar_ref, small_sem.at[4])
    q_copy = pltpu.make_async_copy(q_hbm, q_ref, small_sem.at[5])
    for part in range(parts):
        for i in range(per_part):
            for which in (0, 1):
                local_copy(part, which, i).start()
    for copy in small:
        copy.start()
    q_copy.start()

    barrier = pltpu.get_barrier_semaphore()
    below, above = row > 0, row < rows - 1

    @pl.when(above)
    def _():
        pl.semaphore_signal(
            barrier, inc=1, device_id={"blk": span + 2, "ulysses": core}, device_id_type=MESH
        )

    @pl.when(below)
    def _():
        pl.semaphore_signal(
            barrier, inc=1, device_id={"blk": span - 2, "ulysses": core}, device_id_type=MESH
        )

    for way in (ACROSS, CHIP):
        pl.semaphore_signal(barrier, inc=1, device_id=targets[way], device_id_type=MESH)
    pl.semaphore_wait(barrier, 2 + below.astype(jnp.int32) + above.astype(jnp.int32))

    for part in range(parts):
        pltpu.make_async_copy(piece(part, mine), piece(part, mine), local_sem.at[part]).wait()

        @pl.when(above)
        def _():
            up(part, 0, mine).start()

        @pl.when(below)
        def _():
            across(part, 0, mine).start()

        @pl.when(row == 0)
        def _():
            for i in range(per_part):
                last_across(part * per_part + i, mine).start()

        chip(part, 0, mine, 0).start()

    for copy in small:
        copy.wait()
    key_block = lax.broadcasted_iota(jnp.int32, (groups, 128), 1)
    slashes, verticals = slash_ref[...], vert_ref[...]
    hits = jnp.zeros((groups, 128), jnp.int32)
    for j in range(slashes.shape[1]):
        hits += jnp.where(key_block == mine - slashes[:, j : j + 1], 1, 0)
    for j in range(verticals.shape[1]):
        hits += jnp.where((key_block == verticals[:, j : j + 1]) & (key_block <= mine), 1, 0)
    table_ref[0] = jnp.where(hits > 0, 0.0, -BIG)
    table_ref[1, :, :blocks] = ks_ref[...].astype(jnp.float32) * LOG2E
    query_scales = qs_ref[...].astype(jnp.float32)
    table_ref[2, 0:1, :heads] = jnp.where(core == 0, query_scales[0:1], query_scales[1:2])
    to_scalars.start()

    token = lax.broadcasted_iota(jnp.int32, (BLOCK, BLOCK), 1)
    key_at = lax.broadcasted_iota(jnp.int32, (BLOCK, BLOCK), 0)
    later = jnp.where(key_at > token, 1.0, 0.0)
    eye = jnp.where(key_at == token, 1.0, 0.0).astype(jnp.bfloat16)

    def hidden(block, g):
        own = jnp.where(block == mine, -BIG, 0.0)
        return (scalar_ref[0, g, block] + later * own).astype(jnp.bfloat16)

    def unit(pairs, g, first, last):
        queries = jnp.concatenate(
            [
                jnp.concatenate(
                    [q_ref[:, pl.ds(pl.multiple_of(g * width + p * DH, DH), DH)], eye], axis=1
                )
                for p in range(per_group)
            ],
            axis=0,
        )
        scores, scales = [], []
        for base in pairs:
            keys = kv_ref[g, pl.ds(base, 2), 0].reshape(2 * BLOCK, DH)
            mask = jnp.concatenate([hidden(base, g), hidden(base + 1, g)], axis=0)
            scores.append(
                lax.dot_general(
                    queries,
                    jnp.concatenate([keys, mask], axis=1),
                    (((1,), (1,)), ((), ())),
                    preferred_element_type=jnp.float32,
                )
            )
            scales += [scalar_ref[1, g, base], scalar_ref[1, g, base + 1]]
        probs, alphas = [], []
        for p in range(per_group):
            here = slice(p * BLOCK, (p + 1) * BLOCK)
            q_scale = scalar_ref[2, 0, g * per_group + p]
            tiles = [
                scores[i // 2][here, (i % 2) * BLOCK : (i % 2 + 1) * BLOCK] * (q_scale * scales[i])
                for i in range(2 * len(pairs))
            ]
            top = functools.reduce(jnp.maximum, tiles)
            top = jnp.max(top, axis=1, keepdims=True)
            top = jnp.broadcast_to(top, (BLOCK, DH))
            if not first:
                old = m_ref[g, here, :]
                top = jnp.maximum(old, top)
                alpha = jnp.exp2(old - top)
                alphas.append(alpha)
            weights = [jnp.exp2(tile - top) for tile in tiles]
            total = functools.reduce(jnp.add, weights)
            if not first:
                total = l_ref[g, here, :] * alpha + total
            l_ref[g, here, :] = total
            if not last:
                m_ref[g, here, :] = top
            probs.append(jnp.concatenate([w.astype(jnp.bfloat16) for w in weights], axis=1))
        probs = jnp.concatenate(probs, axis=0)
        held = [kv_ref[g, pl.ds(base, 2), 1].reshape(2 * BLOCK, DH) for base in pairs]
        held = held[0] if len(held) == 1 else jnp.concatenate(held, axis=0)
        added = jnp.dot(probs, held, preferred_element_type=jnp.float32)
        for p in range(per_group):
            here = slice(p * BLOCK, (p + 1) * BLOCK)
            numer = added[here, :]
            if not first:
                numer = acc_ref[g, here, :] * alphas[p] + numer
            if last:
                total = jnp.sum(l_ref[g, here, :], axis=1, keepdims=True)
                o_ref[:, pl.ds(pl.multiple_of(g * width + p * DH, DH), DH)] = (
                    numer * (1.0 / total)
                ).astype(o_ref.dtype)
            else:
                acc_ref[g, here, :] = numer

    q_copy.wait()
    to_scalars.wait()

    @pl.loop(0, parts)
    def _(part):
        chip(part, 0, mine, 0).wait_recv()
        for i in range(per_part):
            unit([block_of(row, col, 0)], part * per_part + i, True, False)

    def pass_on(k, part):
        climbed = block_of(row - k, col, core)
        up(part, k - 1, climbed).wait_recv()

        @pl.when(above)
        def _():
            up(part, k, climbed).start()

        @pl.when(k < row)
        def _():
            across(part, k, climbed).start()

        @pl.when((k == row) & (part < parts // 2))
        def _():
            for i in range(per_part):
                last_across(part * per_part + i, climbed).start()

        chip(part, k, climbed, 0).start()
        crossed = block_of(row - k + 1, 1 - col, core)
        across(part, k - 1, crossed).wait_recv()
        chip(part, k - 1, crossed, 1).start()

    crossed = block_of(0, 1 - col, core)

    def pass_last_on(g):
        last_across(g, crossed).wait_recv()

        @pl.when(above & (g >= half))
        def _():
            last_up(g, crossed).start()

        last_chip(g, crossed).start()

    def last_group(step):
        return step % 2 * half + step // 2

    turns = row * parts

    @pl.loop(0, turns + 1)
    def _(turn):
        @pl.when(turn < turns)
        def _():
            pass_on(1 + turn // parts, turn % parts)

        @pl.when(turn == turns)
        def _():
            pass_last_on(last_group(0))

        @pl.when(turn > 0)
        def _():
            k, part = 1 + (turn - 1) // parts, (turn - 1) % parts
            bases = [block_of(row - k, col, 0), block_of(row - k + 1, 1 - col, 0)]
            both = kv_ref.at[pl.ds(part * per_part, per_part), pl.ds(bases[0], 2)]
            remote(both, CHIP, chip_send.at[0, k], chip_recv.at[part, k]).wait_recv()
            for i in range(per_part):
                unit(bases, part * per_part + i, False, False)

    @pl.loop(0, groups)
    def _(step):
        g = last_group(step)

        @pl.when(step < groups - 1)
        def _():
            pass_last_on(last_group(step + 1))

        last_chip(g, crossed).wait_recv()
        unit([block_of(0, 1 - col, 0)], g, False, True)

    everything = kv_ref.at[:, mine]
    lower = kv_ref.at[pl.ds(0, half), mine]

    @pl.loop(0, row + 1)
    def _(k):
        @pl.when(above)
        def _():
            remote(everything, UP, up_send.at[k], up_recv.at[0, 0]).wait_send()

        @pl.when((k < row) | (row == 0))
        def _():
            remote(everything, ACROSS, across_send.at[k], last_recv.at[0]).wait_send()

        @pl.when((k == row) & below)
        def _():
            remote(lower, ACROSS, across_send.at[k], last_recv.at[0]).wait_send()

        for crossing in (0, 1):
            remote(everything, CHIP, chip_send.at[crossing, k], last_recv.at[0]).wait_send()

    @pl.when(above)
    def _():
        remote(lower, UP, up_send.at[rows], last_recv.at[0]).wait_send()


def attend(mesh, query_int, key_int, values, query_scale, key_scale, verticals, slashes):
    spans = mesh.shape["blk"]
    tokens = query_int.shape[0]
    blocks = key_scale.shape[0]
    heads = query_int.shape[1] // DH
    groups = key_int.shape[1] // DH
    assert tokens == BLOCK and mesh.shape["ulysses"] == 2 and spans % 2 == 0
    assert blocks == spans * 2
    rows = spans // 2
    parts = 4
    assert groups % parts == 0 and parts % 2 == 0 and rows > 1 and max(heads, blocks) <= 128
    per_group = heads // groups
    stack = (groups, per_group * BLOCK, DH)
    hbm = pl.BlockSpec(memory_space=pl.ANY)
    return pl.pallas_call(
        functools.partial(kernel, rows, heads, groups, blocks),
        out_shape=jax.ShapeDtypeStruct(query_int.shape, jnp.bfloat16),
        in_specs=[hbm] * 7,
        out_specs=pl.BlockSpec(memory_space=pltpu.VMEM),
        scratch_shapes=[
            pltpu.VMEM(query_int.shape, jnp.bfloat16),
            pltpu.VMEM((groups, blocks, 2, BLOCK, DH), jnp.bfloat16),
            pltpu.VMEM(stack, jnp.float32),
            pltpu.VMEM(stack, jnp.float32),
            pltpu.VMEM(stack, jnp.float32),
            pltpu.VMEM(query_scale.shape, query_scale.dtype),
            pltpu.VMEM(key_scale.shape[::-1], key_scale.dtype),
            pltpu.VMEM(verticals.shape, jnp.int32),
            pltpu.VMEM(slashes.shape, jnp.int32),
            pltpu.VMEM((3, groups, 128), jnp.float32),
            pltpu.SMEM((3, groups, 128), jnp.float32),
            pltpu.SemaphoreType.DMA((parts,)),
            pltpu.SemaphoreType.DMA((6,)),
            pltpu.SemaphoreType.DMA((rows + 1,)),
            pltpu.SemaphoreType.DMA((rows,)),
            pltpu.SemaphoreType.DMA((2, rows)),
            pltpu.SemaphoreType.DMA((parts, rows - 1)),
            pltpu.SemaphoreType.DMA((parts, rows - 1)),
            pltpu.SemaphoreType.DMA((parts, rows)),
            pltpu.SemaphoreType.DMA((groups,)),
            pltpu.SemaphoreType.DMA((groups,)),
        ],
        compiler_params=pltpu.CompilerParams(
            collective_id=0, has_side_effects=True, vmem_limit_bytes=(20 + blocks // 2) * 1024 * 1024
        ),
    )(*[pltpu.with_memory_space_constraint(x, pltpu.HBM) for x in (query_int, key_int, values, query_scale, key_scale.T, verticals, slashes)])


def solution(mesh):
    in_specs = (
        P(("group", "blk", "ulysses"), None),
        P(("group", "blk", "ulysses"), None),
        P(("group", "blk", "ulysses"), None),
        P(("group", "blk"), None),
        P("group", None),
        P("group", None),
        P("group", None),
    )
    out_specs = P(("group", "blk", "ulysses"), None)
    return jax.shard_map(
        functools.partial(attend, mesh),
        mesh=mesh,
        in_specs=in_specs,
        out_specs=out_specs,
        check_vma=False,
    )
```

```python
import functools
import math

import jax
import jax.numpy as jnp
from jax import lax
from jax.experimental import pallas as pl
from jax.experimental.pallas import tpu as pltpu
from jax.sharding import PartitionSpec as P

BLOCK = 128
DH = 128
BIG = 2.0**40
LOG2E = math.log2(math.e)
MESH = pl.DeviceIdType.MESH
UP, ACROSS, CHIP = 0, 1, 2


def kernel(
    rows, heads, groups, blocks, q_hbm, k_hbm, v_hbm, qs_hbm, ks_hbm, vert_hbm, slash_hbm, o_ref,
    q_ref, kv_ref, m_ref, l_ref, acc_ref, qs_ref, ks_ref, vert_ref, slash_ref,
    table_ref, scalar_ref, local_sem, small_sem,
    up_send, across_send, chip_send, up_recv, across_recv, chip_recv, last_recv, chip_last_recv,
):
    span = lax.axis_index("blk")
    core = lax.axis_index("ulysses")
    row, col = span // 2, span % 2
    mine = span * 2 + core
    per_group = heads // groups
    width = per_group * DH
    parts = local_sem.shape[0]
    per_part = groups // parts
    half = groups // 2

    def block_of(r, c, u):
        return (r * 2 + c) * 2 + u

    targets = {
        UP: {"blk": span + 2, "ulysses": core},
        ACROSS: {"blk": row * 2 + 1 - col, "ulysses": core},
        CHIP: {"blk": span, "ulysses": 1 - core},
    }

    def remote(place, way, send_sem, recv_sem):
        return pltpu.make_async_remote_copy(
            src_ref=place,
            dst_ref=place,
            send_sem=send_sem,
            recv_sem=recv_sem,
            device_id=targets[way],
            device_id_type=MESH,
        )

    def piece(part, block):
        return kv_ref.at[pl.ds(part * per_part, per_part), block]

    def one(g, block):
        return kv_ref.at[pl.ds(g, 1), block]

    def up(part, k, block):
        return remote(piece(part, block), UP, up_send.at[k], up_recv.at[part, k])

    def across(part, k, block):
        return remote(piece(part, block), ACROSS, across_send.at[k], across_recv.at[part, k])

    def chip(part, k, block, crossing):
        return remote(
            piece(part, block), CHIP, chip_send.at[crossing, k], chip_recv.at[part, k + crossing]
        )

    def last_across(g, block):
        return remote(one(g, block), ACROSS, across_send.at[row], last_recv.at[g])

    def last_up(g, block):
        return remote(one(g, block), UP, up_send.at[rows], last_recv.at[g])

    def last_chip(g, block):
        return remote(one(g, block), CHIP, chip_send.at[1, row], chip_last_recv.at[g])

    def local_copy(part, which, i):
        g = part * per_part + i
        return pltpu.make_async_copy(
            (k_hbm, v_hbm)[which].at[:, pl.ds(g * DH, DH)],
            kv_ref.at[g, mine, which],
            local_sem.at[part],
        )

    small = [
        pltpu.make_async_copy(src, dst, small_sem.at[i])
        for i, (src, dst) in enumerate(
            [(qs_hbm, qs_ref), (ks_hbm, ks_ref), (vert_hbm, vert_ref), (slash_hbm, slash_ref)]
        )
    ]
    to_scalars = pltpu.make_async_copy(table_ref, scalar_ref, small_sem.at[4])
    q_copy = pltpu.make_async_copy(q_hbm, q_ref, small_sem.at[5])
    for part in range(parts):
        for i in range(per_part):
            for which in (0, 1):
                local_copy(part, which, i).start()
    for copy in small:
        copy.start()
    q_copy.start()

    barrier = pltpu.get_barrier_semaphore()
    below, above = row > 0, row < rows - 1

    @pl.when(above)
    def _():
        pl.semaphore_signal(
            barrier, inc=1, device_id={"blk": span + 2, "ulysses": core}, device_id_type=MESH
        )

    @pl.when(below)
    def _():
        pl.semaphore_signal(
            barrier, inc=1, device_id={"blk": span - 2, "ulysses": core}, device_id_type=MESH
        )

    for way in (ACROSS, CHIP):
        pl.semaphore_signal(barrier, inc=1, device_id=targets[way], device_id_type=MESH)
    pl.semaphore_wait(barrier, 2 + below.astype(jnp.int32) + above.astype(jnp.int32))

    for part in range(parts):
        pltpu.make_async_copy(piece(part, mine), piece(part, mine), local_sem.at[part]).wait()

        @pl.when(above)
        def _():
            up(part, 0, mine).start()

        @pl.when(below)
        def _():
            across(part, 0, mine).start()

        @pl.when(row == 0)
        def _():
            for i in range(per_part):
                last_across(part * per_part + i, mine).start()

        chip(part, 0, mine, 0).start()

    for copy in small:
        copy.wait()
    key_block = lax.broadcasted_iota(jnp.int32, (groups, 128), 1)
    slashes, verticals = slash_ref[...], vert_ref[...]
    hits = jnp.zeros((groups, 128), jnp.int32)
    for j in range(slashes.shape[1]):
        hits += jnp.where(key_block == mine - slashes[:, j : j + 1], 1, 0)
    for j in range(verticals.shape[1]):
        hits += jnp.where((key_block == verticals[:, j : j + 1]) & (key_block <= mine), 1, 0)
    table_ref[0] = jnp.where(hits > 0, 0.0, -BIG)
    table_ref[1, :, :blocks] = ks_ref[...].astype(jnp.float32) * LOG2E
    query_scales = qs_ref[...].astype(jnp.float32)
    table_ref[2, 0:1, :heads] = jnp.where(core == 0, query_scales[0:1], query_scales[1:2])
    to_scalars.start()

    token = lax.broadcasted_iota(jnp.int32, (BLOCK, BLOCK), 1)
    key_at = lax.broadcasted_iota(jnp.int32, (BLOCK, BLOCK), 0)
    later = jnp.where(key_at > token, 1.0, 0.0)
    eye = jnp.where(key_at == token, 1.0, 0.0).astype(jnp.bfloat16)

    def hidden(block, g):
        own = jnp.where(block == mine, -BIG, 0.0)
        return (scalar_ref[0, g, block] + later * own).astype(jnp.bfloat16)

    def dots(pairs, g):
        queries = jnp.concatenate(
            [
                jnp.concatenate(
                    [q_ref[:, pl.ds(pl.multiple_of(g * width + p * DH, DH), DH)], eye], axis=1
                )
                for p in range(per_group)
            ],
            axis=0,
        )
        scores = []
        for base in pairs:
            keys = kv_ref[g, pl.ds(base, 2), 0].reshape(2 * BLOCK, DH)
            mask = jnp.concatenate([hidden(base, g), hidden(base + 1, g)], axis=0)
            scores.append(
                lax.dot_general(
                    queries,
                    jnp.concatenate([keys, mask], axis=1),
                    (((1,), (1,)), ((), ())),
                    preferred_element_type=jnp.float32,
                )
            )
        return scores

    def unit(pairs, g, scores, first, last):
        scales = [scalar_ref[1, g, base + i] for base in pairs for i in (0, 1)]
        probs, alphas = [], []
        for p in range(per_group):
            here = slice(p * BLOCK, (p + 1) * BLOCK)
            q_scale = scalar_ref[2, 0, g * per_group + p]
            tiles = [
                scores[i // 2][here, (i % 2) * BLOCK : (i % 2 + 1) * BLOCK] * (q_scale * scales[i])
                for i in range(2 * len(pairs))
            ]
            top = functools.reduce(jnp.maximum, tiles)
            top = jnp.max(top, axis=1, keepdims=True)
            top = jnp.broadcast_to(top, (BLOCK, DH))
            if not first:
                old = m_ref[g, here, :]
                top = jnp.maximum(old, top)
                alpha = jnp.exp2(old - top)
                alphas.append(alpha)
            weights = [jnp.exp2(tile - top) for tile in tiles]
            total = functools.reduce(jnp.add, weights)
            if not first:
                total = l_ref[g, here, :] * alpha + total
            l_ref[g, here, :] = total
            if not last:
                m_ref[g, here, :] = top
            probs.append(jnp.concatenate([w.astype(jnp.bfloat16) for w in weights], axis=1))
        probs = jnp.concatenate(probs, axis=0)
        held = [kv_ref[g, pl.ds(base, 2), 1].reshape(2 * BLOCK, DH) for base in pairs]
        held = held[0] if len(held) == 1 else jnp.concatenate(held, axis=0)
        added = jnp.dot(probs, held, preferred_element_type=jnp.float32)
        for p in range(per_group):
            here = slice(p * BLOCK, (p + 1) * BLOCK)
            numer = added[here, :]
            if not first:
                numer = acc_ref[g, here, :] * alphas[p] + numer
            if last:
                total = jnp.sum(l_ref[g, here, :], axis=1, keepdims=True)
                o_ref[:, pl.ds(pl.multiple_of(g * width + p * DH, DH), DH)] = (
                    numer * (1.0 / total)
                ).astype(o_ref.dtype)
            else:
                acc_ref[g, here, :] = numer

    def units(pairs, kv_heads, first, last):
        scores = [dots(pairs, g) for g in kv_heads]
        for g, found in zip(kv_heads, scores):
            unit(pairs, g, found, first, last)

    q_copy.wait()
    to_scalars.wait()

    @pl.loop(0, parts)
    def _(part):
        chip(part, 0, mine, 0).wait_recv()
        units([block_of(row, col, 0)], [part * per_part + i for i in range(per_part)], True, False)

    def pass_on(k, part):
        climbed = block_of(row - k, col, core)
        up(part, k - 1, climbed).wait_recv()

        @pl.when(above)
        def _():
            up(part, k, climbed).start()

        @pl.when(k < row)
        def _():
            across(part, k, climbed).start()

        @pl.when((k == row) & (part < parts // 2))
        def _():
            for i in range(per_part):
                last_across(part * per_part + i, climbed).start()

        chip(part, k, climbed, 0).start()
        crossed = block_of(row - k + 1, 1 - col, core)
        across(part, k - 1, crossed).wait_recv()
        chip(part, k - 1, crossed, 1).start()

    crossed = block_of(0, 1 - col, core)

    def pass_last_on(g):
        last_across(g, crossed).wait_recv()

        @pl.when(above & (g >= half))
        def _():
            last_up(g, crossed).start()

        last_chip(g, crossed).start()

    turns = row * parts

    def climb(turn):
        k, part = 1 + turn // parts, turn % parts
        bases = [block_of(row - k, col, 0), block_of(row - k + 1, 1 - col, 0)]
        return k, part, bases

    def climb_arrived(turn):
        k, part, bases = climb(turn)
        both = kv_ref.at[pl.ds(part * per_part, per_part), pl.ds(bases[0], 2)]
        remote(both, CHIP, chip_send.at[0, k], chip_recv.at[part, k]).wait_recv()

    @pl.loop(0, turns)
    def _(turn):
        pass_on(1 + turn // parts, turn % parts)

        @pl.when(turn > 0)
        def _():
            climb_arrived(turn - 1)
            k, part, bases = climb(turn - 1)
            units(bases, [part * per_part + i for i in range(per_part)], False, False)

    def pass_both_on(step):
        pass_last_on(step)
        pass_last_on(step + half)

    @pl.when(below)
    def _():
        climb_arrived(turns - 1)
        k, part, bases = climb(turns - 1)

        @pl.loop(0, per_part)
        def _(i):
            @pl.when(i == per_part - 1)
            def _():
                pass_both_on(0)

            units(bases, [part * per_part + i], False, False)

    @pl.when(row == 0)
    def _():
        pass_both_on(0)

    @pl.loop(0, half)
    def _(step):
        @pl.when(step < half - 1)
        def _():
            pass_both_on(step + 1)

        for g in (step, step + half):
            last_chip(g, crossed).wait_recv()
        units([block_of(0, 1 - col, 0)], [step, step + half], False, True)

    everything = kv_ref.at[:, mine]
    lower = kv_ref.at[pl.ds(0, half), mine]

    @pl.loop(0, row + 1)
    def _(k):
        @pl.when(above)
        def _():
            remote(everything, UP, up_send.at[k], up_recv.at[0, 0]).wait_send()

        @pl.when((k < row) | (row == 0))
        def _():
            remote(everything, ACROSS, across_send.at[k], last_recv.at[0]).wait_send()

        @pl.when((k == row) & below)
        def _():
            remote(lower, ACROSS, across_send.at[k], last_recv.at[0]).wait_send()

        for crossing in (0, 1):
            remote(everything, CHIP, chip_send.at[crossing, k], last_recv.at[0]).wait_send()

    @pl.when(above)
    def _():
        remote(lower, UP, up_send.at[rows], last_recv.at[0]).wait_send()


def attend(mesh, query_int, key_int, values, query_scale, key_scale, verticals, slashes):
    spans = mesh.shape["blk"]
    tokens = query_int.shape[0]
    blocks = key_scale.shape[0]
    heads = query_int.shape[1] // DH
    groups = key_int.shape[1] // DH
    assert tokens == BLOCK and mesh.shape["ulysses"] == 2 and spans % 2 == 0
    assert blocks == spans * 2
    rows = spans // 2
    parts = 4
    assert groups % parts == 0 and parts % 2 == 0 and rows > 1 and max(heads, blocks) <= 128
    per_group = heads // groups
    stack = (groups, per_group * BLOCK, DH)
    hbm = pl.BlockSpec(memory_space=pl.ANY)
    return pl.pallas_call(
        functools.partial(kernel, rows, heads, groups, blocks),
        out_shape=jax.ShapeDtypeStruct(query_int.shape, jnp.bfloat16),
        in_specs=[hbm] * 7,
        out_specs=pl.BlockSpec(memory_space=pltpu.VMEM),
        scratch_shapes=[
            pltpu.VMEM(query_int.shape, jnp.bfloat16),
            pltpu.VMEM((groups, blocks, 2, BLOCK, DH), jnp.bfloat16),
            pltpu.VMEM(stack, jnp.float32),
            pltpu.VMEM(stack, jnp.float32),
            pltpu.VMEM(stack, jnp.float32),
            pltpu.VMEM(query_scale.shape, query_scale.dtype),
            pltpu.VMEM(key_scale.shape[::-1], key_scale.dtype),
            pltpu.VMEM(verticals.shape, jnp.int32),
            pltpu.VMEM(slashes.shape, jnp.int32),
            pltpu.VMEM((3, groups, 128), jnp.float32),
            pltpu.SMEM((3, groups, 128), jnp.float32),
            pltpu.SemaphoreType.DMA((parts,)),
            pltpu.SemaphoreType.DMA((6,)),
            pltpu.SemaphoreType.DMA((rows + 1,)),
            pltpu.SemaphoreType.DMA((rows,)),
            pltpu.SemaphoreType.DMA((2, rows)),
            pltpu.SemaphoreType.DMA((parts, rows - 1)),
            pltpu.SemaphoreType.DMA((parts, rows - 1)),
            pltpu.SemaphoreType.DMA((parts, rows)),
            pltpu.SemaphoreType.DMA((groups,)),
            pltpu.SemaphoreType.DMA((groups,)),
        ],
        compiler_params=pltpu.CompilerParams(
            collective_id=0, has_side_effects=True, vmem_limit_bytes=(26 + blocks // 2) * 1024 * 1024
        ),
    )(*[pltpu.with_memory_space_constraint(x, pltpu.HBM) for x in (query_int, key_int, values, query_scale, key_scale.T, verticals, slashes)])


def solution(mesh):
    in_specs = (
        P(("group", "blk", "ulysses"), None),
        P(("group", "blk", "ulysses"), None),
        P(("group", "blk", "ulysses"), None),
        P(("group", "blk"), None),
        P("group", None),
        P("group", None),
        P("group", None),
    )
    out_specs = P(("group", "blk", "ulysses"), None)
    return jax.shard_map(
        functools.partial(attend, mesh),
        mesh=mesh,
        in_specs=in_specs,
        out_specs=out_specs,
        check_vma=False,
    )
```

```python
import functools
import math

import jax
import jax.numpy as jnp
from jax import lax
from jax.experimental import pallas as pl
from jax.experimental.pallas import tpu as pltpu
from jax.sharding import PartitionSpec as P

BLOCK = 128
DH = 128
BIG = 2.0**40
LOG2E = math.log2(math.e)
MESH = pl.DeviceIdType.MESH
UP, ACROSS, CHIP = 0, 1, 2


def kernel(
    rows, heads, groups, blocks, q_hbm, k_hbm, v_hbm, qs_hbm, ks_hbm, vert_hbm, slash_hbm, o_ref,
    q_ref, kv_ref, m_ref, l_ref, acc_ref, qs_ref, ks_ref, vert_ref, slash_ref,
    table_ref, scalar_ref, local_sem, small_sem,
    up_send, across_send, chip_send, up_recv, across_recv, pair_recv, chip_recv, last_recv,
    chip_last_recv,
):
    span = lax.axis_index("blk")
    core = lax.axis_index("ulysses")
    row, col = span // 2, span % 2
    mine = span * 2 + core
    per_group = heads // groups
    width = per_group * DH
    parts = local_sem.shape[0]
    per_part = groups // parts
    half = groups // 2

    def block_of(r, c, u):
        return (r * 2 + c) * 2 + u

    targets = {
        UP: {"blk": span + 2, "ulysses": core},
        ACROSS: {"blk": row * 2 + 1 - col, "ulysses": core},
        CHIP: {"blk": span, "ulysses": 1 - core},
    }

    def remote(place, way, send_sem, recv_sem):
        return pltpu.make_async_remote_copy(
            src_ref=place,
            dst_ref=place,
            send_sem=send_sem,
            recv_sem=recv_sem,
            device_id=targets[way],
            device_id_type=MESH,
        )

    def piece(part, block):
        return kv_ref.at[pl.ds(part * per_part, per_part), block]

    def one(g, block):
        return kv_ref.at[pl.ds(g, 1), block]

    def up(part, k, block):
        return remote(piece(part, block), UP, up_send.at[0], up_recv.at[part, k])

    def across(part, k, block):
        return remote(piece(part, block), ACROSS, across_send.at[0], across_recv.at[part, k])

    def chip_own(part):
        return remote(piece(part, mine), CHIP, chip_send.at[0], pair_recv.at[0])

    def chip(part, k, block):
        return remote(piece(part, block), CHIP, chip_send.at[0], chip_recv.at[part, k - 1])

    def last_across(g, block):
        return remote(one(g, block), ACROSS, across_send.at[1], last_recv.at[g])

    def last_up(g, block):
        return remote(one(g, block), UP, up_send.at[1], last_recv.at[g])

    def last_chip(g, block):
        return remote(one(g, block), CHIP, chip_send.at[0], chip_last_recv.at[g % half])

    def local_copy(part, which, i):
        g = part * per_part + i
        return pltpu.make_async_copy(
            (k_hbm, v_hbm)[which].at[:, pl.ds(g * DH, DH)],
            kv_ref.at[g, mine, which],
            local_sem.at[part],
        )

    small = [
        pltpu.make_async_copy(src, dst, small_sem.at[i])
        for i, (src, dst) in enumerate(
            [(qs_hbm, qs_ref), (ks_hbm, ks_ref), (vert_hbm, vert_ref), (slash_hbm, slash_ref)]
        )
    ]
    to_scalars = pltpu.make_async_copy(table_ref, scalar_ref, small_sem.at[4])
    q_copy = pltpu.make_async_copy(q_hbm, q_ref, small_sem.at[5])
    for part in range(parts):
        for i in range(per_part):
            for which in (0, 1):
                local_copy(part, which, i).start()
    for copy in small:
        copy.start()
    q_copy.start()

    barrier = pltpu.get_barrier_semaphore()
    below, above = row > 0, row < rows - 1

    @pl.when(above)
    def _():
        pl.semaphore_signal(
            barrier, inc=1, device_id={"blk": span + 2, "ulysses": core}, device_id_type=MESH
        )

    @pl.when(below)
    def _():
        pl.semaphore_signal(
            barrier, inc=1, device_id={"blk": span - 2, "ulysses": core}, device_id_type=MESH
        )

    for way in (ACROSS, CHIP):
        pl.semaphore_signal(barrier, inc=1, device_id=targets[way], device_id_type=MESH)
    pl.semaphore_wait(barrier, 2 + below.astype(jnp.int32) + above.astype(jnp.int32))

    for part in range(parts):
        pltpu.make_async_copy(piece(part, mine), piece(part, mine), local_sem.at[part]).wait()

        @pl.when(above)
        def _():
            up(part, 0, mine).start()

        @pl.when(below)
        def _():
            across(part, 0, mine).start()

        @pl.when(row == 0)
        def _():
            for i in range(per_part):
                last_across(part * per_part + i, mine).start()

        chip_own(part).start()

    for copy in small:
        copy.wait()
    key_block = lax.broadcasted_iota(jnp.int32, (groups, 128), 1)
    slashes, verticals = slash_ref[...], vert_ref[...]
    hits = jnp.zeros((groups, 128), jnp.int32)
    for j in range(slashes.shape[1]):
        hits += jnp.where(key_block == mine - slashes[:, j : j + 1], 1, 0)
    for j in range(verticals.shape[1]):
        hits += jnp.where((key_block == verticals[:, j : j + 1]) & (key_block <= mine), 1, 0)
    table_ref[0] = jnp.where(hits > 0, 0.0, -BIG)
    table_ref[1, :, :blocks] = ks_ref[...].astype(jnp.float32) * LOG2E
    query_scales = qs_ref[...].astype(jnp.float32)
    table_ref[2, 0:1, :heads] = jnp.where(core == 0, query_scales[0:1], query_scales[1:2])
    to_scalars.start()

    token = lax.broadcasted_iota(jnp.int32, (BLOCK, BLOCK), 1)
    key_at = lax.broadcasted_iota(jnp.int32, (BLOCK, BLOCK), 0)
    later = jnp.where(key_at > token, 1.0, 0.0)
    eye = jnp.where(key_at == token, 1.0, 0.0).astype(jnp.bfloat16)

    def hidden(block, g):
        own = jnp.where(block == mine, -BIG, 0.0)
        return (scalar_ref[0, g, block] + later * own).astype(jnp.bfloat16)

    def dots(pairs, g, first):
        queries = jnp.concatenate(
            [
                jnp.concatenate(
                    [q_ref[:, pl.ds(pl.multiple_of(g * width + p * DH, DH), DH)], eye], axis=1
                )
                for p in range(per_group)
            ],
            axis=0,
        )
        scores = []
        for base in pairs:
            keys = kv_ref[g, pl.ds(base, 2), 0].reshape(2 * BLOCK, DH)
            masks = [
                hidden(base + i, g) if first
                else jnp.full((BLOCK, BLOCK), scalar_ref[0, g, base + i], jnp.float32).astype(jnp.bfloat16)
                for i in (0, 1)
            ]
            mask = jnp.concatenate(masks, axis=0)
            scores.append(
                lax.dot_general(
                    queries,
                    jnp.concatenate([keys, mask], axis=1),
                    (((1,), (1,)), ((), ())),
                    preferred_element_type=jnp.float32,
                )
            )
        return scores

    def unit(pairs, g, scores, first, last):
        scales = [scalar_ref[1, g, base + i] for base in pairs for i in (0, 1)]
        probs, alphas = [], []
        for p in range(per_group):
            here = slice(p * BLOCK, (p + 1) * BLOCK)
            q_scale = scalar_ref[2, 0, g * per_group + p]
            tiles = [
                scores[i // 2][here, (i % 2) * BLOCK : (i % 2 + 1) * BLOCK] * (q_scale * scales[i])
                for i in range(2 * len(pairs))
            ]
            top = functools.reduce(jnp.maximum, tiles)
            top = jnp.max(top, axis=1, keepdims=True)
            top = jnp.broadcast_to(top, (BLOCK, DH))
            if not first:
                old = m_ref[g, here, :]
                top = jnp.maximum(old, top)
                alpha = jnp.exp2(old - top)
                alphas.append(alpha)
            weights = [jnp.exp2(tile - top) for tile in tiles]
            total = functools.reduce(jnp.add, weights)
            if not first:
                total = l_ref[g, here, :] * alpha + total
            l_ref[g, here, :] = total
            if not last:
                m_ref[g, here, :] = top
            probs.append(jnp.concatenate([w.astype(jnp.bfloat16) for w in weights], axis=1))
        probs = jnp.concatenate(probs, axis=0)
        held = [kv_ref[g, pl.ds(base, 2), 1].reshape(2 * BLOCK, DH) for base in pairs]
        held = held[0] if len(held) == 1 else jnp.concatenate(held, axis=0)
        added = jnp.dot(probs, held, preferred_element_type=jnp.float32)
        for p in range(per_group):
            here = slice(p * BLOCK, (p + 1) * BLOCK)
            numer = added[here, :]
            if not first:
                numer = acc_ref[g, here, :] * alphas[p] + numer
            if last:
                total = jnp.sum(l_ref[g, here, :], axis=1, keepdims=True)
                o_ref[:, pl.ds(pl.multiple_of(g * width + p * DH, DH), DH)] = (
                    numer * (1.0 / total)
                ).astype(o_ref.dtype)
            else:
                acc_ref[g, here, :] = numer

    def units(pairs, kv_heads, first, last):
        scores = [dots(pairs, g, first) for g in kv_heads]
        for g, found in zip(kv_heads, scores):
            unit(pairs, g, found, first, last)

    q_copy.wait()
    to_scalars.wait()

    everything = kv_ref.at[:, mine]
    remote(everything, CHIP, chip_send.at[0], pair_recv.at[0]).wait_recv()

    @pl.loop(0, parts)
    def _(part):
        units([block_of(row, col, 0)], [part * per_part + i for i in range(per_part)], True, False)

    def pass_on(k, part):
        climbed = block_of(row - k, col, core)
        up(part, k - 1, climbed).wait_recv()

        chip(part, k, climbed).start()

        @pl.when(above)
        def _():
            up(part, k, climbed).start()

        @pl.when(k < row)
        def _():
            across(part, k, climbed).start()

        @pl.when(k == row)
        def _():
            for i in range(per_part):
                g = part * per_part + i

                @pl.when(g < half)
                def _():
                    last_across(g, climbed).start()

        crossed = block_of(row - k + 1, 1 - col, core)
        across(part, k - 1, crossed).wait_recv()
        chip(part, k, crossed).start()

    crossed = block_of(0, 1 - col, core)

    def pass_last_on(g):
        last_across(g, crossed).wait_recv()

        last_chip(g, crossed).start()

        @pl.when(above & (g >= half))
        def _():
            last_up(g, crossed).start()

    turns = row * parts

    def climb(turn):
        k, part = 1 + turn // parts, turn % parts
        bases = [block_of(row - k, col, 0), block_of(row - k + 1, 1 - col, 0)]
        return k, part, bases

    def climb_arrived(turn):
        k, part, bases = climb(turn)
        both = kv_ref.at[pl.ds(part * per_part, per_part), pl.ds(bases[0], 2)]
        remote(both, CHIP, chip_send.at[0], chip_recv.at[part, k - 1]).wait_recv()

    @pl.loop(0, turns)
    def _(turn):
        pass_on(1 + turn // parts, turn % parts)

        @pl.when(turn > 0)
        def _():
            climb_arrived(turn - 1)
            k, part, bases = climb(turn - 1)
            units(bases, [part * per_part + i for i in range(per_part)], False, False)

    def pass_both_on(step):
        pass_last_on(step + half)
        pass_last_on(step)

    @pl.when(below)
    def _():
        climb_arrived(turns - 1)
        k, part, bases = climb(turns - 1)

        pass_both_on(0)
        units(bases, [part * per_part + i for i in range(per_part)], False, False)

    @pl.when(row == 0)
    def _():
        pass_both_on(0)

    @pl.loop(0, half)
    def _(step):
        @pl.when(step < half - 1)
        def _():
            pass_both_on(step + 1)

        two = kv_ref.at[pl.ds(0, 2), crossed]
        remote(two, CHIP, chip_send.at[0], chip_last_recv.at[step]).wait_recv()
        units([block_of(0, 1 - col, 0)], [step, step + half], False, True)

    def sent(place, way, sem):
        remote(place, way, sem, pair_recv.at[0]).wait_send()

    lower = kv_ref.at[pl.ds(0, half), mine]

    @pl.when(below)
    def _():
        sent(lower, ACROSS, across_send.at[1])

    @pl.when(above)
    def _():
        sent(lower, UP, up_send.at[1])

    for r in range(rows):

        @pl.when(row == r)
        def _():
            if r == 0:
                sent(everything, ACROSS, across_send.at[1])
            else:
                sent(kv_ref.at[:, pl.ds(0, r)], ACROSS, across_send.at[0])
            if r < rows - 1:
                sent(kv_ref.at[:, pl.ds(0, r + 1)], UP, up_send.at[0])
            sent(kv_ref.at[:, pl.ds(0, 2 * r + 2)], CHIP, chip_send.at[0])


def attend(mesh, query_int, key_int, values, query_scale, key_scale, verticals, slashes):
    spans = mesh.shape["blk"]
    tokens = query_int.shape[0]
    blocks = key_scale.shape[0]
    heads = query_int.shape[1] // DH
    groups = key_int.shape[1] // DH
    assert tokens == BLOCK and mesh.shape["ulysses"] == 2 and spans % 2 == 0
    assert blocks == spans * 2
    rows = spans // 2
    parts = 4
    assert groups % parts == 0 and groups % 2 == 0 and parts % 2 == 0 and rows > 1 and max(heads, blocks) <= 128
    per_group = heads // groups
    stack = (groups, per_group * BLOCK, DH)
    hbm = pl.BlockSpec(memory_space=pl.ANY)
    return pl.pallas_call(
        functools.partial(kernel, rows, heads, groups, blocks),
        out_shape=jax.ShapeDtypeStruct(query_int.shape, jnp.bfloat16),
        in_specs=[hbm] * 7,
        out_specs=pl.BlockSpec(memory_space=pltpu.VMEM),
        scratch_shapes=[
            pltpu.VMEM(query_int.shape, jnp.bfloat16),
            pltpu.VMEM((groups, blocks, 2, BLOCK, DH), jnp.bfloat16),
            pltpu.VMEM(stack, jnp.float32),
            pltpu.VMEM(stack, jnp.float32),
            pltpu.VMEM(stack, jnp.float32),
            pltpu.VMEM(query_scale.shape, query_scale.dtype),
            pltpu.VMEM(key_scale.shape[::-1], key_scale.dtype),
            pltpu.VMEM(verticals.shape, jnp.int32),
            pltpu.VMEM(slashes.shape, jnp.int32),
            pltpu.VMEM((3, groups, 128), jnp.float32),
            pltpu.SMEM((3, groups, 128), jnp.float32),
            pltpu.SemaphoreType.DMA((parts,)),
            pltpu.SemaphoreType.DMA((6,)),
            pltpu.SemaphoreType.DMA((2,)),
            pltpu.SemaphoreType.DMA((2,)),
            pltpu.SemaphoreType.DMA((1,)),
            pltpu.SemaphoreType.DMA((parts, rows - 1)),
            pltpu.SemaphoreType.DMA((parts, rows - 1)),
            pltpu.SemaphoreType.DMA((1,)),
            pltpu.SemaphoreType.DMA((parts, rows - 1)),
            pltpu.SemaphoreType.DMA((groups,)),
            pltpu.SemaphoreType.DMA((groups // 2,)),
        ],
        compiler_params=pltpu.CompilerParams(
            collective_id=0, has_side_effects=True, vmem_limit_bytes=(26 + blocks // 2) * 1024 * 1024
        ),
    )(*[pltpu.with_memory_space_constraint(x, pltpu.HBM) for x in (query_int, key_int, values, query_scale, key_scale.T, verticals, slashes)])


def solution(mesh):
    in_specs = (
        P(("group", "blk", "ulysses"), None),
        P(("group", "blk", "ulysses"), None),
        P(("group", "blk", "ulysses"), None),
        P(("group", "blk"), None),
        P("group", None),
        P("group", None),
        P("group", None),
    )
    out_specs = P(("group", "blk", "ulysses"), None)
    return jax.shard_map(
        functools.partial(attend, mesh),
        mesh=mesh,
        in_specs=in_specs,
        out_specs=out_specs,
        check_vma=False,
    )
```

```python
import functools
import math

import jax
import jax.numpy as jnp
from jax import lax
from jax.experimental import pallas as pl
from jax.experimental.pallas import tpu as pltpu
from jax.sharding import PartitionSpec as P

BLOCK = 128
DH = 128
BIG = 2.0**40
LOG2E = math.log2(math.e)
MESH = pl.DeviceIdType.MESH
UP, ACROSS, CHIP = 0, 1, 2


def kernel(
    rows, heads, groups, blocks, q_hbm, k_hbm, v_hbm, qs_hbm, ks_hbm, vert_hbm, slash_hbm, o_ref,
    q_ref, kv_ref, m_ref, l_ref, acc_ref, qs_ref, ks_ref, vert_ref, slash_ref,
    table_ref, scalar_ref, local_sem, small_sem,
    up_send, across_send, chip_send, up_recv, across_recv, pair_recv, chip_recv, last_recv,
    chip_last_recv,
):
    span = lax.axis_index("blk")
    core = lax.axis_index("ulysses")
    row, col = span // 2, span % 2
    mine = span * 2 + core
    per_group = heads // groups
    width = per_group * DH
    parts = local_sem.shape[0]
    per_part = groups // parts
    half = groups // 2

    def block_of(r, c, u):
        return (r * 2 + c) * 2 + u

    targets = {
        UP: {"blk": span + 2, "ulysses": core},
        ACROSS: {"blk": row * 2 + 1 - col, "ulysses": core},
        CHIP: {"blk": span, "ulysses": 1 - core},
    }

    def remote(place, way, send_sem, recv_sem):
        return pltpu.make_async_remote_copy(
            src_ref=place,
            dst_ref=place,
            send_sem=send_sem,
            recv_sem=recv_sem,
            device_id=targets[way],
            device_id_type=MESH,
        )

    def piece(part, block):
        return kv_ref.at[pl.ds(part * per_part, per_part), block]

    def one(g, block):
        return kv_ref.at[pl.ds(g, 1), block]

    def up(part, k, block):
        return remote(piece(part, block), UP, up_send.at[0], up_recv.at[part, k])

    def across(part, k, block):
        return remote(piece(part, block), ACROSS, across_send.at[0], across_recv.at[part, k])

    def chip_own(part):
        return remote(piece(part, mine), CHIP, chip_send.at[0], pair_recv.at[0])

    def chip(part, k, block):
        return remote(piece(part, block), CHIP, chip_send.at[0], chip_recv.at[part, k - 1])

    def last_across(g, block):
        return remote(one(g, block), ACROSS, across_send.at[1], last_recv.at[g])

    def last_up(g, block):
        return remote(one(g, block), UP, up_send.at[1], last_recv.at[g])

    def last_chip(g, block):
        return remote(one(g, block), CHIP, chip_send.at[0], chip_last_recv.at[g % half])

    def local_copy(part, which, i):
        g = part * per_part + i
        return pltpu.make_async_copy(
            (k_hbm, v_hbm)[which].at[:, pl.ds(g * DH, DH)],
            kv_ref.at[g, mine, which],
            local_sem.at[part],
        )

    small = [
        pltpu.make_async_copy(src, dst, small_sem.at[i])
        for i, (src, dst) in enumerate(
            [(qs_hbm, qs_ref), (ks_hbm, ks_ref), (vert_hbm, vert_ref), (slash_hbm, slash_ref)]
        )
    ]
    to_scalars = pltpu.make_async_copy(table_ref, scalar_ref, small_sem.at[4])
    q_copy = pltpu.make_async_copy(q_hbm, q_ref, small_sem.at[5])
    barrier = pltpu.get_barrier_semaphore()
    below, above = row > 0, row < rows - 1

    @pl.when(above)
    def _():
        pl.semaphore_signal(
            barrier, inc=1, device_id={"blk": span + 2, "ulysses": core}, device_id_type=MESH
        )

    @pl.when(below)
    def _():
        pl.semaphore_signal(
            barrier, inc=1, device_id={"blk": span - 2, "ulysses": core}, device_id_type=MESH
        )

    for way in (ACROSS, CHIP):
        pl.semaphore_signal(barrier, inc=1, device_id=targets[way], device_id_type=MESH)
    for part in range(parts):
        for i in range(per_part):
            for which in (0, 1):
                local_copy(part, which, i).start()
    for copy in small:
        copy.start()
    pl.semaphore_wait(barrier, 2 + below.astype(jnp.int32) + above.astype(jnp.int32))

    for part in range(parts):
        pltpu.make_async_copy(piece(part, mine), piece(part, mine), local_sem.at[part]).wait()

        @pl.when(above)
        def _():
            up(part, 0, mine).start()

        @pl.when(below)
        def _():
            across(part, 0, mine).start()

        @pl.when(row == 0)
        def _():
            for i in range(per_part):
                last_across(part * per_part + i, mine).start()

        chip_own(part).start()

    q_copy.start()
    for copy in small:
        copy.wait()
    key_block = lax.broadcasted_iota(jnp.int32, (groups, 128), 1)
    slashes, verticals = slash_ref[...], vert_ref[...]
    hits = jnp.zeros((groups, 128), jnp.int32)
    for j in range(slashes.shape[1]):
        hits += jnp.where(key_block == mine - slashes[:, j : j + 1], 1, 0)
    for j in range(verticals.shape[1]):
        hits += jnp.where((key_block == verticals[:, j : j + 1]) & (key_block <= mine), 1, 0)
    table_ref[0] = jnp.where(hits > 0, 0.0, -BIG)
    table_ref[1, :, :blocks] = ks_ref[...].astype(jnp.float32) * LOG2E
    query_scales = qs_ref[...].astype(jnp.float32)
    table_ref[2, 0:1, :heads] = jnp.where(core == 0, query_scales[0:1], query_scales[1:2])
    to_scalars.start()

    token = lax.broadcasted_iota(jnp.int32, (BLOCK, BLOCK), 1)
    key_at = lax.broadcasted_iota(jnp.int32, (BLOCK, BLOCK), 0)
    later = jnp.where(key_at > token, 1.0, 0.0)
    eye = jnp.where(key_at == token, 1.0, 0.0).astype(jnp.bfloat16)

    def hidden(block, g):
        own = jnp.where(block == mine, -BIG, 0.0)
        return (scalar_ref[0, g, block] + later * own).astype(jnp.bfloat16)

    def dots(pairs, g, first):
        queries = jnp.concatenate(
            [
                jnp.concatenate(
                    [q_ref[:, pl.ds(pl.multiple_of(g * width + p * DH, DH), DH)], eye], axis=1
                )
                for p in range(per_group)
            ],
            axis=0,
        )
        scores = []
        for base in pairs:
            keys = kv_ref[g, pl.ds(base, 2), 0].reshape(2 * BLOCK, DH)
            masks = [
                hidden(base + i, g) if first
                else jnp.full((BLOCK, BLOCK), scalar_ref[0, g, base + i], jnp.float32).astype(jnp.bfloat16)
                for i in (0, 1)
            ]
            mask = jnp.concatenate(masks, axis=0)
            scores.append(
                lax.dot_general(
                    queries,
                    jnp.concatenate([keys, mask], axis=1),
                    (((1,), (1,)), ((), ())),
                    preferred_element_type=jnp.float32,
                )
            )
        return scores

    def unit(pairs, g, scores, first, last):
        scales = [scalar_ref[1, g, base + i] for base in pairs for i in (0, 1)]
        probs, alphas = [], []
        for p in range(per_group):
            here = slice(p * BLOCK, (p + 1) * BLOCK)
            q_scale = scalar_ref[2, 0, g * per_group + p]
            tiles = [
                scores[i // 2][here, (i % 2) * BLOCK : (i % 2 + 1) * BLOCK] * (q_scale * scales[i])
                for i in range(2 * len(pairs))
            ]
            top = functools.reduce(jnp.maximum, tiles)
            top = jnp.max(top, axis=1, keepdims=True)
            top = jnp.broadcast_to(top, (BLOCK, DH))
            if not first:
                old = m_ref[g, here, :]
                top = jnp.maximum(old, top)
                alpha = jnp.exp2(old - top)
                alphas.append(alpha)
            weights = [jnp.exp2(tile - top) for tile in tiles]
            total = functools.reduce(jnp.add, weights)
            if not first:
                total = l_ref[g, here, :] * alpha + total
            l_ref[g, here, :] = total
            if not last:
                m_ref[g, here, :] = top
            probs.append(jnp.concatenate([w.astype(jnp.bfloat16) for w in weights], axis=1))
        probs = jnp.concatenate(probs, axis=0)
        held = [kv_ref[g, pl.ds(base, 2), 1].reshape(2 * BLOCK, DH) for base in pairs]
        held = held[0] if len(held) == 1 else jnp.concatenate(held, axis=0)
        added = jnp.dot(probs, held, preferred_element_type=jnp.float32)
        for p in range(per_group):
            here = slice(p * BLOCK, (p + 1) * BLOCK)
            numer = added[here, :]
            if not first:
                numer = acc_ref[g, here, :] * alphas[p] + numer
            if last:
                total = jnp.sum(l_ref[g, here, :], axis=1, keepdims=True)
                o_ref[:, pl.ds(pl.multiple_of(g * width + p * DH, DH), DH)] = (
                    numer * (1.0 / total)
                ).astype(o_ref.dtype)
            else:
                acc_ref[g, here, :] = numer

    def units(pairs, kv_heads, first, last):
        scores = [dots(pairs, g, first) for g in kv_heads]
        for g, found in zip(kv_heads, scores):
            unit(pairs, g, found, first, last)

    q_copy.wait()
    to_scalars.wait()

    everything = kv_ref.at[:, mine]
    remote(everything, CHIP, chip_send.at[0], pair_recv.at[0]).wait_recv()

    @pl.loop(0, parts)
    def _(part):
        units([block_of(row, col, 0)], [part * per_part + i for i in range(per_part)], True, False)

    def pass_on(k, part):
        climbed = block_of(row - k, col, core)
        up(part, k - 1, climbed).wait_recv()

        chip(part, k, climbed).start()

        @pl.when(above)
        def _():
            up(part, k, climbed).start()

        @pl.when(k < row)
        def _():
            across(part, k, climbed).start()

        @pl.when(k == row)
        def _():
            for i in range(per_part):
                g = part * per_part + i

                @pl.when(g < half)
                def _():
                    last_across(g, climbed).start()

        crossed = block_of(row - k + 1, 1 - col, core)
        across(part, k - 1, crossed).wait_recv()
        chip(part, k, crossed).start()

    crossed = block_of(0, 1 - col, core)

    def pass_last_on(g):
        last_across(g, crossed).wait_recv()

        last_chip(g, crossed).start()

        @pl.when(above & (g >= half))
        def _():
            last_up(g, crossed).start()

    turns = row * parts

    def climb(turn):
        k, part = 1 + turn // parts, turn % parts
        bases = [block_of(row - k, col, 0), block_of(row - k + 1, 1 - col, 0)]
        return k, part, bases

    def climb_arrived(turn):
        k, part, bases = climb(turn)
        both = kv_ref.at[pl.ds(part * per_part, per_part), pl.ds(bases[0], 2)]
        remote(both, CHIP, chip_send.at[0], chip_recv.at[part, k - 1]).wait_recv()

    @pl.loop(0, turns)
    def _(turn):
        pass_on(1 + turn // parts, turn % parts)

        @pl.when(turn > 0)
        def _():
            climb_arrived(turn - 1)
            k, part, bases = climb(turn - 1)
            units(bases, [part * per_part + i for i in range(per_part)], False, False)

    def pass_both_on(step):
        pass_last_on(step + half)
        pass_last_on(step)

    @pl.when(below)
    def _():
        climb_arrived(turns - 1)
        k, part, bases = climb(turns - 1)

        pass_both_on(0)
        units(bases, [part * per_part + i for i in range(per_part)], False, False)

    @pl.when(row == 0)
    def _():
        pass_both_on(0)

    @pl.loop(0, half)
    def _(step):
        @pl.when(step < half - 1)
        def _():
            pass_both_on(step + 1)

        two = kv_ref.at[pl.ds(0, 2), crossed]
        remote(two, CHIP, chip_send.at[0], chip_last_recv.at[step]).wait_recv()
        units([block_of(0, 1 - col, 0)], [step, step + half], False, True)

    def sent(place, way, sem):
        remote(place, way, sem, pair_recv.at[0]).wait_send()

    lower = kv_ref.at[pl.ds(0, half), mine]

    @pl.when(below)
    def _():
        sent(lower, ACROSS, across_send.at[1])

    @pl.when(above)
    def _():
        sent(lower, UP, up_send.at[1])

    for r in range(rows):

        @pl.when(row == r)
        def _():
            if r == 0:
                sent(everything, ACROSS, across_send.at[1])
            else:
                sent(kv_ref.at[:, pl.ds(0, r)], ACROSS, across_send.at[0])
            if r < rows - 1:
                sent(kv_ref.at[:, pl.ds(0, r + 1)], UP, up_send.at[0])
            sent(kv_ref.at[:, pl.ds(0, 2 * r + 2)], CHIP, chip_send.at[0])


def attend(mesh, query_int, key_int, values, query_scale, key_scale, verticals, slashes):
    spans = mesh.shape["blk"]
    tokens = query_int.shape[0]
    blocks = key_scale.shape[0]
    heads = query_int.shape[1] // DH
    groups = key_int.shape[1] // DH
    assert tokens == BLOCK and mesh.shape["ulysses"] == 2 and spans % 2 == 0
    assert blocks == spans * 2
    rows = spans // 2
    parts = 4
    assert groups % parts == 0 and groups % 2 == 0 and parts % 2 == 0 and rows > 1 and max(heads, blocks) <= 128
    per_group = heads // groups
    stack = (groups, per_group * BLOCK, DH)
    hbm = pl.BlockSpec(memory_space=pl.ANY)
    return pl.pallas_call(
        functools.partial(kernel, rows, heads, groups, blocks),
        out_shape=jax.ShapeDtypeStruct(query_int.shape, jnp.bfloat16),
        in_specs=[hbm] * 7,
        out_specs=pl.BlockSpec(memory_space=pltpu.VMEM),
        scratch_shapes=[
            pltpu.VMEM(query_int.shape, jnp.bfloat16),
            pltpu.VMEM((groups, blocks, 2, BLOCK, DH), jnp.bfloat16),
            pltpu.VMEM(stack, jnp.float32),
            pltpu.VMEM(stack, jnp.float32),
            pltpu.VMEM(stack, jnp.float32),
            pltpu.VMEM(query_scale.shape, query_scale.dtype),
            pltpu.VMEM(key_scale.shape[::-1], key_scale.dtype),
            pltpu.VMEM(verticals.shape, jnp.int32),
            pltpu.VMEM(slashes.shape, jnp.int32),
            pltpu.VMEM((3, groups, 128), jnp.float32),
            pltpu.SMEM((3, groups, 128), jnp.float32),
            pltpu.SemaphoreType.DMA((parts,)),
            pltpu.SemaphoreType.DMA((6,)),
            pltpu.SemaphoreType.DMA((2,)),
            pltpu.SemaphoreType.DMA((2,)),
            pltpu.SemaphoreType.DMA((1,)),
            pltpu.SemaphoreType.DMA((parts, rows - 1)),
            pltpu.SemaphoreType.DMA((parts, rows - 1)),
            pltpu.SemaphoreType.DMA((1,)),
            pltpu.SemaphoreType.DMA((parts, rows - 1)),
            pltpu.SemaphoreType.DMA((groups,)),
            pltpu.SemaphoreType.DMA((groups // 2,)),
        ],
        compiler_params=pltpu.CompilerParams(
            collective_id=0, has_side_effects=True, vmem_limit_bytes=(26 + blocks // 2) * 1024 * 1024
        ),
    )(*[pltpu.with_memory_space_constraint(x, pltpu.HBM) for x in (query_int, key_int, values, query_scale, key_scale.T, verticals, slashes)])


def solution(mesh):
    in_specs = (
        P(("group", "blk", "ulysses"), None),
        P(("group", "blk", "ulysses"), None),
        P(("group", "blk", "ulysses"), None),
        P(("group", "blk"), None),
        P("group", None),
        P("group", None),
        P("group", None),
    )
    out_specs = P(("group", "blk", "ulysses"), None)
    return jax.shard_map(
        functools.partial(attend, mesh),
        mesh=mesh,
        in_specs=in_specs,
        out_specs=out_specs,
        check_vma=False,
    )
```

```python
import functools
import math

import jax
import jax.numpy as jnp
from jax import lax
from jax.experimental import pallas as pl
from jax.experimental.pallas import tpu as pltpu
from jax.sharding import PartitionSpec as P

BLOCK = 128
DH = 128
BIG = 2.0**40
LOG2E = math.log2(math.e)
MESH = pl.DeviceIdType.MESH
UP, ACROSS, CHIP = 0, 1, 2


def kernel(
    rows, heads, groups, blocks, q_hbm, k_hbm, v_hbm, qs_hbm, ks_hbm, vert_hbm, slash_hbm, o_ref,
    q_ref, kv_ref, m_ref, l_ref, acc_ref, qs_ref, ks_ref, vert_ref, slash_ref,
    table_ref, scalar_ref, local_sem, small_sem,
    up_send, across_send, chip_send, up_recv, across_recv, pair_recv, chip_recv, last_recv,
    chip_last_recv,
):
    span = lax.axis_index("blk")
    core = lax.axis_index("ulysses")
    row, col = span // 2, span % 2
    mine = span * 2 + core
    per_group = heads // groups
    width = per_group * DH
    parts = local_sem.shape[0]
    per_part = groups // parts
    half = groups // 2

    def block_of(r, c, u):
        return (r * 2 + c) * 2 + u

    targets = {
        UP: {"blk": span + 2, "ulysses": core},
        ACROSS: {"blk": row * 2 + 1 - col, "ulysses": core},
        CHIP: {"blk": span, "ulysses": 1 - core},
    }

    def remote(place, way, send_sem, recv_sem):
        return pltpu.make_async_remote_copy(
            src_ref=place,
            dst_ref=place,
            send_sem=send_sem,
            recv_sem=recv_sem,
            device_id=targets[way],
            device_id_type=MESH,
        )

    def piece(part, block):
        return kv_ref.at[pl.ds(part * per_part, per_part), block]

    def one(g, block):
        return kv_ref.at[pl.ds(g, 1), block]

    def up(part, k, block):
        return remote(piece(part, block), UP, up_send.at[0], up_recv.at[part, k])

    def across(part, k, block):
        return remote(piece(part, block), ACROSS, across_send.at[0], across_recv.at[part, k])

    def chip_own(part):
        return remote(piece(part, mine), CHIP, chip_send.at[0], pair_recv.at[0])

    def chip(part, k, block):
        return remote(piece(part, block), CHIP, chip_send.at[0], chip_recv.at[part, k - 1])

    def last_across(g, block):
        return remote(one(g, block), ACROSS, across_send.at[1], last_recv.at[g])

    def last_up(g, block):
        return remote(one(g, block), UP, up_send.at[1], last_recv.at[g])

    def last_chip(g, block):
        return remote(one(g, block), CHIP, chip_send.at[0], chip_last_recv.at[g % half])

    def local_copy(part, which, i):
        g = part * per_part + i
        return pltpu.make_async_copy(
            (k_hbm, v_hbm)[which].at[:, pl.ds(g * DH, DH)],
            kv_ref.at[g, mine, which],
            local_sem.at[part],
        )

    small = [
        pltpu.make_async_copy(src, dst, small_sem.at[i])
        for i, (src, dst) in enumerate(
            [(qs_hbm, qs_ref), (ks_hbm, ks_ref), (vert_hbm, vert_ref), (slash_hbm, slash_ref)]
        )
    ]
    to_scalars = pltpu.make_async_copy(table_ref, scalar_ref, small_sem.at[4])
    q_copy = pltpu.make_async_copy(q_hbm, q_ref, small_sem.at[5])
    barrier = pltpu.get_barrier_semaphore()
    below, above = row > 0, row < rows - 1

    @pl.when(above)
    def _():
        pl.semaphore_signal(
            barrier, inc=1, device_id={"blk": span + 2, "ulysses": core}, device_id_type=MESH
        )

    @pl.when(below)
    def _():
        pl.semaphore_signal(
            barrier, inc=1, device_id={"blk": span - 2, "ulysses": core}, device_id_type=MESH
        )

    for way in (ACROSS, CHIP):
        pl.semaphore_signal(barrier, inc=1, device_id=targets[way], device_id_type=MESH)
    for part in range(parts):
        for i in range(per_part):
            for which in (0, 1):
                local_copy(part, which, i).start()
    for copy in small:
        copy.start()
    pl.semaphore_wait(barrier, 2 + below.astype(jnp.int32) + above.astype(jnp.int32))

    for part in range(parts):
        pltpu.make_async_copy(piece(part, mine), piece(part, mine), local_sem.at[part]).wait()

        @pl.when(above)
        def _():
            up(part, 0, mine).start()

        @pl.when(below & (col == 0))
        def _():
            across(part, 0, mine).start()

        @pl.when(row == 0)
        def _():
            for i in range(per_part):
                last_across(part * per_part + i, mine).start()

        chip_own(part).start()

    q_copy.start()
    for copy in small:
        copy.wait()
    key_block = lax.broadcasted_iota(jnp.int32, (groups, 128), 1)
    slashes, verticals = slash_ref[...], vert_ref[...]
    hits = jnp.zeros((groups, 128), jnp.int32)
    for j in range(slashes.shape[1]):
        hits += jnp.where(key_block == mine - slashes[:, j : j + 1], 1, 0)
    for j in range(verticals.shape[1]):
        hits += jnp.where((key_block == verticals[:, j : j + 1]) & (key_block <= mine), 1, 0)
    table_ref[0] = jnp.where(hits > 0, 0.0, -BIG)
    table_ref[1, :, :blocks] = ks_ref[...].astype(jnp.float32) * LOG2E
    query_scales = qs_ref[...].astype(jnp.float32)
    table_ref[2, 0:1, :heads] = jnp.where(core == 0, query_scales[0:1], query_scales[1:2])
    to_scalars.start()

    token = lax.broadcasted_iota(jnp.int32, (BLOCK, BLOCK), 1)
    key_at = lax.broadcasted_iota(jnp.int32, (BLOCK, BLOCK), 0)
    later = jnp.where(key_at > token, 1.0, 0.0)
    eye = jnp.where(key_at == token, 1.0, 0.0).astype(jnp.bfloat16)

    def hidden(block, g):
        own = jnp.where(block == mine, -BIG, 0.0)
        return (scalar_ref[0, g, block] + later * own).astype(jnp.bfloat16)

    def dots(pairs, g, first):
        queries = jnp.concatenate(
            [
                jnp.concatenate(
                    [q_ref[:, pl.ds(pl.multiple_of(g * width + p * DH, DH), DH)], eye], axis=1
                )
                for p in range(per_group)
            ],
            axis=0,
        )
        scores = []
        for base in pairs:
            keys = kv_ref[g, pl.ds(base, 2), 0].reshape(2 * BLOCK, DH)
            masks = [
                hidden(base + i, g) if first
                else jnp.full((BLOCK, BLOCK), scalar_ref[0, g, base + i], jnp.float32).astype(jnp.bfloat16)
                for i in (0, 1)
            ]
            mask = jnp.concatenate(masks, axis=0)
            scores.append(
                lax.dot_general(
                    queries,
                    jnp.concatenate([keys, mask], axis=1),
                    (((1,), (1,)), ((), ())),
                    preferred_element_type=jnp.float32,
                )
            )
        return scores

    def unit(pairs, g, scores, first, last):
        scales = [scalar_ref[1, g, base + i] for base in pairs for i in (0, 1)]
        probs, alphas = [], []
        for p in range(per_group):
            here = slice(p * BLOCK, (p + 1) * BLOCK)
            q_scale = scalar_ref[2, 0, g * per_group + p]
            tiles = [
                scores[i // 2][here, (i % 2) * BLOCK : (i % 2 + 1) * BLOCK] * (q_scale * scales[i])
                for i in range(2 * len(pairs))
            ]
            top = functools.reduce(jnp.maximum, tiles)
            top = jnp.max(top, axis=1, keepdims=True)
            top = jnp.broadcast_to(top, (BLOCK, DH))
            if not first:
                old = m_ref[g, here, :]
                top = jnp.maximum(old, top)
                alpha = jnp.exp2(old - top)
                alphas.append(alpha)
            weights = [jnp.exp2(tile - top) for tile in tiles]
            total = functools.reduce(jnp.add, weights)
            if not first:
                total = l_ref[g, here, :] * alpha + total
            l_ref[g, here, :] = total
            if not last:
                m_ref[g, here, :] = top
            probs.append(jnp.concatenate([w.astype(jnp.bfloat16) for w in weights], axis=1))
        probs = jnp.concatenate(probs, axis=0)
        held = [kv_ref[g, pl.ds(base, 2), 1].reshape(2 * BLOCK, DH) for base in pairs]
        held = held[0] if len(held) == 1 else jnp.concatenate(held, axis=0)
        added = jnp.dot(probs, held, preferred_element_type=jnp.float32)
        for p in range(per_group):
            here = slice(p * BLOCK, (p + 1) * BLOCK)
            numer = added[here, :]
            if not first:
                numer = acc_ref[g, here, :] * alphas[p] + numer
            if last:
                total = jnp.sum(l_ref[g, here, :], axis=1, keepdims=True)
                o_ref[:, pl.ds(pl.multiple_of(g * width + p * DH, DH), DH)] = (
                    numer * (1.0 / total)
                ).astype(o_ref.dtype)
            else:
                acc_ref[g, here, :] = numer

    def units(pairs, kv_heads, first, last):
        scores = [dots(pairs, g, first) for g in kv_heads]
        for g, found in zip(kv_heads, scores):
            unit(pairs, g, found, first, last)

    q_copy.wait()
    to_scalars.wait()

    everything = kv_ref.at[:, mine]
    remote(everything, CHIP, chip_send.at[0], pair_recv.at[0]).wait_recv()

    @pl.loop(0, parts)
    def _(part):
        units([block_of(row, col, 0)], [part * per_part + i for i in range(per_part)], True, False)

    def pass_on(k, part):
        climbed = block_of(row - k, col, core)
        up(part, k - 1, climbed).wait_recv()

        chip(part, k, climbed).start()

        @pl.when(above)
        def _():
            up(part, k, climbed).start()

        @pl.when(k < row)
        def _():
            across(part, k, climbed).start()

        @pl.when(k == row)
        def _():
            for i in range(per_part):
                g = part * per_part + i

                @pl.when(g < half)
                def _():
                    last_across(g, climbed).start()

        crossed = block_of(row - k + 1, 1 - col, core)

        @pl.when((k > 1) | (col == 1))
        def _():
            across(part, k - 1, crossed).wait_recv()
            chip(part, k, crossed).start()

    crossed = block_of(0, 1 - col, core)

    def pass_last_on(g):
        last_across(g, crossed).wait_recv()

        last_chip(g, crossed).start()

        @pl.when(above & (g >= half))
        def _():
            last_up(g, crossed).start()

    turns = row * parts

    def climb(turn):
        k, part = 1 + turn // parts, turn % parts
        bases = [block_of(row - k, col, 0), block_of(row - k + 1, 1 - col, 0)]
        return k, part, bases

    def climb_arrived(turn):
        k, part, bases = climb(turn)
        both = kv_ref.at[pl.ds(part * per_part, per_part), pl.ds(bases[0], 2)]

        @pl.when((k > 1) | (col == 1))
        def _():
            remote(both, CHIP, chip_send.at[0], chip_recv.at[part, k - 1]).wait_recv()

        @pl.when((k == 1) & (col == 0))
        def _():
            chip(part, k, bases[0]).wait_recv()

    @pl.loop(0, turns)
    def _(turn):
        pass_on(1 + turn // parts, turn % parts)

        @pl.when(turn > 0)
        def _():
            climb_arrived(turn - 1)
            k, part, bases = climb(turn - 1)
            kv_heads = [part * per_part + i for i in range(per_part)]

            @pl.when((k > 1) | (col == 1))
            def _():
                units(bases, kv_heads, False, False)

            @pl.when((k == 1) & (col == 0))
            def _():
                units(bases[:1], kv_heads, False, False)

    def pass_both_on(step):
        pass_last_on(step + half)
        pass_last_on(step)

    @pl.when(below)
    def _():
        climb_arrived(turns - 1)
        k, part, bases = climb(turns - 1)

        pass_both_on(0)
        kv_heads = [part * per_part + i for i in range(per_part)]

        @pl.when((k > 1) | (col == 1))
        def _():
            units(bases, kv_heads, False, False)

        @pl.when((k == 1) & (col == 0))
        def _():
            units(bases[:1], kv_heads, False, False)

    @pl.when(row == 0)
    def _():
        pass_both_on(0)

    @pl.loop(0, half)
    def _(step):
        @pl.when(step < half - 1)
        def _():
            pass_both_on(step + 1)

        two = kv_ref.at[pl.ds(0, 2), crossed]
        remote(two, CHIP, chip_send.at[0], chip_last_recv.at[step]).wait_recv()
        units([block_of(0, 1 - col, 0)], [step, step + half], False, True)

    def sent(place, way, sem):
        remote(place, way, sem, pair_recv.at[0]).wait_send()

    lower = kv_ref.at[pl.ds(0, half), mine]

    @pl.when(below)
    def _():
        sent(lower, ACROSS, across_send.at[1])

    @pl.when(above)
    def _():
        sent(lower, UP, up_send.at[1])

    for r in range(rows):

        @pl.when(row == r)
        def _():
            if r == 0:
                sent(everything, ACROSS, across_send.at[1])
            else:
                @pl.when(col == 0)
                def _():
                    sent(kv_ref.at[:, pl.ds(0, r)], ACROSS, across_send.at[0])

                if r > 1:

                    @pl.when(col == 1)
                    def _():
                        sent(kv_ref.at[:, pl.ds(0, r - 1)], ACROSS, across_send.at[0])
            if r < rows - 1:
                sent(kv_ref.at[:, pl.ds(0, r + 1)], UP, up_send.at[0])
            for c in (0, 1):
                blocks_sent = 2 * r + 2 - (c == 0 and r > 0)

                @pl.when(col == c)
                def _():
                    sent(kv_ref.at[:, pl.ds(0, blocks_sent)], CHIP, chip_send.at[0])


def attend(mesh, query_int, key_int, values, query_scale, key_scale, verticals, slashes):
    spans = mesh.shape["blk"]
    tokens = query_int.shape[0]
    blocks = key_scale.shape[0]
    heads = query_int.shape[1] // DH
    groups = key_int.shape[1] // DH
    assert tokens == BLOCK and mesh.shape["ulysses"] == 2 and spans % 2 == 0
    assert blocks == spans * 2
    rows = spans // 2
    parts = 4
    assert groups % parts == 0 and groups % 2 == 0 and parts % 2 == 0 and rows > 1 and max(heads, blocks) <= 128
    per_group = heads // groups
    stack = (groups, per_group * BLOCK, DH)
    hbm = pl.BlockSpec(memory_space=pl.ANY)
    return pl.pallas_call(
        functools.partial(kernel, rows, heads, groups, blocks),
        out_shape=jax.ShapeDtypeStruct(query_int.shape, jnp.bfloat16),
        in_specs=[hbm] * 7,
        out_specs=pl.BlockSpec(memory_space=pltpu.VMEM),
        scratch_shapes=[
            pltpu.VMEM(query_int.shape, jnp.bfloat16),
            pltpu.VMEM((groups, blocks, 2, BLOCK, DH), jnp.bfloat16),
            pltpu.VMEM(stack, jnp.float32),
            pltpu.VMEM(stack, jnp.float32),
            pltpu.VMEM(stack, jnp.float32),
            pltpu.VMEM(query_scale.shape, query_scale.dtype),
            pltpu.VMEM(key_scale.shape[::-1], key_scale.dtype),
            pltpu.VMEM(verticals.shape, jnp.int32),
            pltpu.VMEM(slashes.shape, jnp.int32),
            pltpu.VMEM((3, groups, 128), jnp.float32),
            pltpu.SMEM((3, groups, 128), jnp.float32),
            pltpu.SemaphoreType.DMA((parts,)),
            pltpu.SemaphoreType.DMA((6,)),
            pltpu.SemaphoreType.DMA((2,)),
            pltpu.SemaphoreType.DMA((2,)),
            pltpu.SemaphoreType.DMA((1,)),
            pltpu.SemaphoreType.DMA((parts, rows - 1)),
            pltpu.SemaphoreType.DMA((parts, rows - 1)),
            pltpu.SemaphoreType.DMA((1,)),
            pltpu.SemaphoreType.DMA((parts, rows - 1)),
            pltpu.SemaphoreType.DMA((groups,)),
            pltpu.SemaphoreType.DMA((groups // 2,)),
        ],
        compiler_params=pltpu.CompilerParams(
            collective_id=0, has_side_effects=True, vmem_limit_bytes=(26 + blocks // 2) * 1024 * 1024
        ),
    )(*[pltpu.with_memory_space_constraint(x, pltpu.HBM) for x in (query_int, key_int, values, query_scale, key_scale.T, verticals, slashes)])


def solution(mesh):
    in_specs = (
        P(("group", "blk", "ulysses"), None),
        P(("group", "blk", "ulysses"), None),
        P(("group", "blk", "ulysses"), None),
        P(("group", "blk"), None),
        P("group", None),
        P("group", None),
        P("group", None),
    )
    out_specs = P(("group", "blk", "ulysses"), None)
    return jax.shard_map(
        functools.partial(attend, mesh),
        mesh=mesh,
        in_specs=in_specs,
        out_specs=out_specs,
        check_vma=False,
    )
```

```python
import functools
import math

import jax
import jax.numpy as jnp
from jax import lax
from jax.experimental import pallas as pl
from jax.experimental.pallas import tpu as pltpu
from jax.sharding import PartitionSpec as P

BLOCK = 128
DH = 128
BIG = 2.0**40
LOG2E = math.log2(math.e)
MESH = pl.DeviceIdType.MESH
UP, ACROSS, CHIP = 0, 1, 2


def kernel(
    rows, heads, groups, blocks, q_hbm, k_hbm, v_hbm, qs_hbm, ks_hbm, vert_hbm, slash_hbm, o_ref,
    q_ref, kv_ref, m_ref, l_ref, acc_ref, qs_ref, ks_ref, vert_ref, slash_ref,
    table_ref, scalar_ref, local_sem, small_sem,
    up_send, across_send, chip_send, up_recv, across_recv, pair_recv, chip_recv, last_recv,
    chip_last_recv,
):
    span = lax.axis_index("blk")
    core = lax.axis_index("ulysses")
    row, col = span // 2, span % 2
    mine = span * 2 + core
    per_group = heads // groups
    width = per_group * DH
    parts = local_sem.shape[0]
    per_part = groups // parts
    half = groups // 2

    def block_of(r, c, u):
        return (r * 2 + c) * 2 + u

    targets = {
        UP: {"blk": span + 2, "ulysses": core},
        ACROSS: {"blk": row * 2 + 1 - col, "ulysses": core},
        CHIP: {"blk": span, "ulysses": 1 - core},
    }

    def remote(place, way, send_sem, recv_sem):
        return pltpu.make_async_remote_copy(
            src_ref=place,
            dst_ref=place,
            send_sem=send_sem,
            recv_sem=recv_sem,
            device_id=targets[way],
            device_id_type=MESH,
        )

    def piece(part, block):
        return kv_ref.at[pl.ds(part * per_part, per_part), block]

    def one(g, block):
        return kv_ref.at[pl.ds(g, 1), block]

    def up(part, k, block):
        return remote(piece(part, block), UP, up_send.at[0], up_recv.at[part, k])

    def across(part, k, block):
        return remote(piece(part, block), ACROSS, across_send.at[0], across_recv.at[part, k])

    def chip_own(part):
        return remote(piece(part, mine), CHIP, chip_send.at[0], pair_recv.at[0])

    def chip(part, k, block):
        return remote(piece(part, block), CHIP, chip_send.at[0], chip_recv.at[part, k - 1])

    def last_across(g, block):
        return remote(one(g, block), ACROSS, across_send.at[1], last_recv.at[g])

    def last_up(g, block):
        return remote(one(g, block), UP, up_send.at[1], last_recv.at[g])

    def last_chip(g, block):
        return remote(one(g, block), CHIP, chip_send.at[0], chip_last_recv.at[g % half])

    def local_copy(part, which, i):
        g = part * per_part + i
        return pltpu.make_async_copy(
            (k_hbm, v_hbm)[which].at[:, pl.ds(g * DH, DH)],
            kv_ref.at[g, mine, which],
            local_sem.at[part],
        )

    small = [
        pltpu.make_async_copy(src, dst, small_sem.at[i])
        for i, (src, dst) in enumerate(
            [(qs_hbm, qs_ref), (ks_hbm, ks_ref), (vert_hbm, vert_ref), (slash_hbm, slash_ref)]
        )
    ]
    to_scalars = pltpu.make_async_copy(table_ref, scalar_ref, small_sem.at[4])
    q_copy = pltpu.make_async_copy(q_hbm, q_ref, small_sem.at[5])
    barrier = pltpu.get_barrier_semaphore()
    below, above = row > 0, row < rows - 1

    @pl.when(below)
    def _():
        pl.semaphore_signal(
            barrier, inc=1, device_id={"blk": span - 2, "ulysses": core}, device_id_type=MESH
        )

    for way in (ACROSS, CHIP):
        pl.semaphore_signal(barrier, inc=1, device_id=targets[way], device_id_type=MESH)
    for part in range(parts):
        for i in range(per_part):
            for which in (0, 1):
                local_copy(part, which, i).start()
    for copy in small:
        copy.start()
    pl.semaphore_wait(barrier, 2 + above.astype(jnp.int32))

    for part in range(parts):
        pltpu.make_async_copy(piece(part, mine), piece(part, mine), local_sem.at[part]).wait()

        @pl.when(above)
        def _():
            up(part, 0, mine).start()

        @pl.when(below & (col == 0))
        def _():
            across(part, 0, mine).start()

        @pl.when(row == 0)
        def _():
            for i in range(per_part):
                last_across(part * per_part + i, mine).start()

        chip_own(part).start()

    q_copy.start()
    for copy in small:
        copy.wait()
    key_block = lax.broadcasted_iota(jnp.int32, (groups, 128), 1)
    slashes, verticals = slash_ref[...], vert_ref[...]
    hits = jnp.zeros((groups, 128), jnp.int32)
    for j in range(slashes.shape[1]):
        hits += jnp.where(key_block == mine - slashes[:, j : j + 1], 1, 0)
    for j in range(verticals.shape[1]):
        hits += jnp.where((key_block == verticals[:, j : j + 1]) & (key_block <= mine), 1, 0)
    table_ref[0] = jnp.where(hits > 0, 0.0, -BIG)
    table_ref[1, :, :blocks] = ks_ref[...].astype(jnp.float32) * LOG2E
    query_scales = qs_ref[...].astype(jnp.float32)
    table_ref[2, 0:1, :heads] = jnp.where(core == 0, query_scales[0:1], query_scales[1:2])
    to_scalars.start()

    token = lax.broadcasted_iota(jnp.int32, (BLOCK, BLOCK), 1)
    key_at = lax.broadcasted_iota(jnp.int32, (BLOCK, BLOCK), 0)
    later = jnp.where(key_at > token, 1.0, 0.0)
    eye = jnp.where(key_at == token, 1.0, 0.0).astype(jnp.bfloat16)

    def hidden(block, g):
        own = jnp.where(block == mine, -BIG, 0.0)
        return (scalar_ref[0, g, block] + later * own).astype(jnp.bfloat16)

    def dots(pairs, g, first):
        queries = jnp.concatenate(
            [
                jnp.concatenate(
                    [q_ref[:, pl.ds(pl.multiple_of(g * width + p * DH, DH), DH)], eye], axis=1
                )
                for p in range(per_group)
            ],
            axis=0,
        )
        scores = []
        for base in pairs:
            keys = kv_ref[g, pl.ds(base, 2), 0].reshape(2 * BLOCK, DH)
            masks = [
                hidden(base + i, g) if first
                else jnp.full((BLOCK, BLOCK), scalar_ref[0, g, base + i], jnp.float32).astype(jnp.bfloat16)
                for i in (0, 1)
            ]
            mask = jnp.concatenate(masks, axis=0)
            scores.append(
                lax.dot_general(
                    queries,
                    jnp.concatenate([keys, mask], axis=1),
                    (((1,), (1,)), ((), ())),
                    preferred_element_type=jnp.float32,
                )
            )
        return scores

    def unit(pairs, g, scores, first, last):
        scales = [scalar_ref[1, g, base + i] for base in pairs for i in (0, 1)]
        probs, alphas = [], []
        for p in range(per_group):
            here = slice(p * BLOCK, (p + 1) * BLOCK)
            q_scale = scalar_ref[2, 0, g * per_group + p]
            tiles = [
                scores[i // 2][here, (i % 2) * BLOCK : (i % 2 + 1) * BLOCK] * (q_scale * scales[i])
                for i in range(2 * len(pairs))
            ]
            top = functools.reduce(jnp.maximum, tiles)
            top = jnp.max(top, axis=1, keepdims=True)
            top = jnp.broadcast_to(top, (BLOCK, DH))
            if not first:
                old = m_ref[g, here, :]
                top = jnp.maximum(old, top)
                alpha = jnp.exp2(old - top)
                alphas.append(alpha)
            weights = [jnp.exp2(tile - top) for tile in tiles]
            total = functools.reduce(jnp.add, weights)
            if not first:
                total = l_ref[g, here, :] * alpha + total
            l_ref[g, here, :] = total
            if not last:
                m_ref[g, here, :] = top
            probs.append(jnp.concatenate([w.astype(jnp.bfloat16) for w in weights], axis=1))
        probs = jnp.concatenate(probs, axis=0)
        held = [kv_ref[g, pl.ds(base, 2), 1].reshape(2 * BLOCK, DH) for base in pairs]
        held = held[0] if len(held) == 1 else jnp.concatenate(held, axis=0)
        added = jnp.dot(probs, held, preferred_element_type=jnp.float32)
        for p in range(per_group):
            here = slice(p * BLOCK, (p + 1) * BLOCK)
            numer = added[here, :]
            if not first:
                numer = acc_ref[g, here, :] * alphas[p] + numer
            if last:
                total = jnp.sum(l_ref[g, here, :], axis=1, keepdims=True)
                o_ref[:, pl.ds(pl.multiple_of(g * width + p * DH, DH), DH)] = (
                    numer * (1.0 / total)
                ).astype(o_ref.dtype)
            else:
                acc_ref[g, here, :] = numer

    def units(pairs, kv_heads, first, last):
        scores = [dots(pairs, g, first) for g in kv_heads]
        for g, found in zip(kv_heads, scores):
            unit(pairs, g, found, first, last)

    q_copy.wait()
    to_scalars.wait()

    everything = kv_ref.at[:, mine]
    remote(everything, CHIP, chip_send.at[0], pair_recv.at[0]).wait_recv()

    @pl.loop(0, parts)
    def _(part):
        units([block_of(row, col, 0)], [part * per_part + i for i in range(per_part)], True, False)

    def pass_on(k, part):
        climbed = block_of(row - k, col, core)
        up(part, k - 1, climbed).wait_recv()

        chip(part, k, climbed).start()

        @pl.when(above)
        def _():
            up(part, k, climbed).start()

        @pl.when(k < row)
        def _():
            across(part, k, climbed).start()

        @pl.when(k == row)
        def _():
            for i in range(per_part):
                g = part * per_part + i

                @pl.when(g < half)
                def _():
                    last_across(g, climbed).start()

        crossed = block_of(row - k + 1, 1 - col, core)

        @pl.when((k > 1) | (col == 1))
        def _():
            across(part, k - 1, crossed).wait_recv()
            chip(part, k, crossed).start()

    crossed = block_of(0, 1 - col, core)

    def pass_last_on(g):
        last_across(g, crossed).wait_recv()

        last_chip(g, crossed).start()

        @pl.when(above & (g >= half))
        def _():
            last_up(g, crossed).start()

    turns = row * parts

    def climb(turn):
        k, part = 1 + turn // parts, turn % parts
        bases = [block_of(row - k, col, 0), block_of(row - k + 1, 1 - col, 0)]
        return k, part, bases

    def climb_arrived(turn):
        k, part, bases = climb(turn)
        both = kv_ref.at[pl.ds(part * per_part, per_part), pl.ds(bases[0], 2)]

        @pl.when((k > 1) | (col == 1))
        def _():
            remote(both, CHIP, chip_send.at[0], chip_recv.at[part, k - 1]).wait_recv()

        @pl.when((k == 1) & (col == 0))
        def _():
            chip(part, k, bases[0]).wait_recv()

    @pl.loop(0, turns)
    def _(turn):
        pass_on(1 + turn // parts, turn % parts)

        @pl.when(turn > 0)
        def _():
            climb_arrived(turn - 1)
            k, part, bases = climb(turn - 1)
            kv_heads = [part * per_part + i for i in range(per_part)]

            @pl.when((k > 1) | (col == 1))
            def _():
                units(bases, kv_heads, False, False)

            @pl.when((k == 1) & (col == 0))
            def _():
                units(bases[:1], kv_heads, False, False)

    def pass_both_on(step):
        pass_last_on(step + half)
        pass_last_on(step)

    @pl.when(below)
    def _():
        climb_arrived(turns - 1)
        k, part, bases = climb(turns - 1)

        pass_both_on(0)
        kv_heads = [part * per_part + i for i in range(per_part)]

        @pl.when((k > 1) | (col == 1))
        def _():
            units(bases, kv_heads, False, False)

        @pl.when((k == 1) & (col == 0))
        def _():
            units(bases[:1], kv_heads, False, False)

    @pl.when(row == 0)
    def _():
        pass_both_on(0)

    @pl.loop(0, half)
    def _(step):
        @pl.when(step < half - 1)
        def _():
            pass_both_on(step + 1)

        two = kv_ref.at[pl.ds(0, 2), crossed]
        remote(two, CHIP, chip_send.at[0], chip_last_recv.at[step]).wait_recv()
        units([block_of(0, 1 - col, 0)], [step, step + half], False, True)

    def sent(place, way, sem):
        remote(place, way, sem, pair_recv.at[0]).wait_send()

    lower = kv_ref.at[pl.ds(0, half), mine]

    @pl.when(below)
    def _():
        sent(lower, ACROSS, across_send.at[1])

    @pl.when(above)
    def _():
        sent(lower, UP, up_send.at[1])

    for r in range(rows):

        @pl.when(row == r)
        def _():
            if r == 0:
                sent(everything, ACROSS, across_send.at[1])
            else:
                @pl.when(col == 0)
                def _():
                    sent(kv_ref.at[:, pl.ds(0, r)], ACROSS, across_send.at[0])

                if r > 1:

                    @pl.when(col == 1)
                    def _():
                        sent(kv_ref.at[:, pl.ds(0, r - 1)], ACROSS, across_send.at[0])
            if r < rows - 1:
                sent(kv_ref.at[:, pl.ds(0, r + 1)], UP, up_send.at[0])
            for c in (0, 1):
                blocks_sent = 2 * r + 2 - (c == 0 and r > 0)

                @pl.when(col == c)
                def _():
                    sent(kv_ref.at[:, pl.ds(0, blocks_sent)], CHIP, chip_send.at[0])


def attend(mesh, query_int, key_int, values, query_scale, key_scale, verticals, slashes):
    spans = mesh.shape["blk"]
    tokens = query_int.shape[0]
    blocks = key_scale.shape[0]
    heads = query_int.shape[1] // DH
    groups = key_int.shape[1] // DH
    assert tokens == BLOCK and mesh.shape["ulysses"] == 2 and spans % 2 == 0
    assert blocks == spans * 2
    rows = spans // 2
    parts = 4
    assert groups % parts == 0 and groups % 2 == 0 and parts % 2 == 0 and rows > 1 and max(heads, blocks) <= 128
    per_group = heads // groups
    stack = (groups, per_group * BLOCK, DH)
    hbm = pl.BlockSpec(memory_space=pl.ANY)
    return pl.pallas_call(
        functools.partial(kernel, rows, heads, groups, blocks),
        out_shape=jax.ShapeDtypeStruct(query_int.shape, jnp.bfloat16),
        in_specs=[hbm] * 7,
        out_specs=pl.BlockSpec(memory_space=pltpu.VMEM),
        scratch_shapes=[
            pltpu.VMEM(query_int.shape, jnp.bfloat16),
            pltpu.VMEM((groups, blocks, 2, BLOCK, DH), jnp.bfloat16),
            pltpu.VMEM(stack, jnp.float32),
            pltpu.VMEM(stack, jnp.float32),
            pltpu.VMEM(stack, jnp.float32),
            pltpu.VMEM(query_scale.shape, query_scale.dtype),
            pltpu.VMEM(key_scale.shape[::-1], key_scale.dtype),
            pltpu.VMEM(verticals.shape, jnp.int32),
            pltpu.VMEM(slashes.shape, jnp.int32),
            pltpu.VMEM((3, groups, 128), jnp.float32),
            pltpu.SMEM((3, groups, 128), jnp.float32),
            pltpu.SemaphoreType.DMA((parts,)),
            pltpu.SemaphoreType.DMA((6,)),
            pltpu.SemaphoreType.DMA((2,)),
            pltpu.SemaphoreType.DMA((2,)),
            pltpu.SemaphoreType.DMA((1,)),
            pltpu.SemaphoreType.DMA((parts, rows - 1)),
            pltpu.SemaphoreType.DMA((parts, rows - 1)),
            pltpu.SemaphoreType.DMA((1,)),
            pltpu.SemaphoreType.DMA((parts, rows - 1)),
            pltpu.SemaphoreType.DMA((groups,)),
            pltpu.SemaphoreType.DMA((groups // 2,)),
        ],
        compiler_params=pltpu.CompilerParams(
            collective_id=0, has_side_effects=True, vmem_limit_bytes=(26 + blocks // 2) * 1024 * 1024
        ),
    )(*[pltpu.with_memory_space_constraint(x, pltpu.HBM) for x in (query_int, key_int, values, query_scale, key_scale.T, verticals, slashes)])


def solution(mesh):
    in_specs = (
        P(("group", "blk", "ulysses"), None),
        P(("group", "blk", "ulysses"), None),
        P(("group", "blk", "ulysses"), None),
        P(("group", "blk"), None),
        P("group", None),
        P("group", None),
        P("group", None),
    )
    out_specs = P(("group", "blk", "ulysses"), None)
    return jax.shard_map(
        functools.partial(attend, mesh),
        mesh=mesh,
        in_specs=in_specs,
        out_specs=out_specs,
        check_vma=False,
    )
```

```python
import functools
import math

import jax
import jax.numpy as jnp
from jax import lax
from jax.experimental import pallas as pl
from jax.experimental.pallas import tpu as pltpu
from jax.sharding import PartitionSpec as P

BLOCK = 128
DH = 128
BIG = 2.0**40
LOG2E = math.log2(math.e)
MESH = pl.DeviceIdType.MESH
UP, ACROSS, CHIP = 0, 1, 2


def kernel(
    rows, heads, groups, blocks, q_hbm, k_hbm, v_hbm, qs_hbm, ks_hbm, vert_hbm, slash_hbm, o_ref,
    q_ref, kv_ref, m_ref, l_ref, acc_ref, qs_ref, ks_ref, vert_ref, slash_ref,
    table_ref, scalar_ref, local_sem, small_sem,
    up_send, across_send, chip_send, up_recv, across_recv, pair_recv, chip_recv, last_recv,
    chip_last_recv,
):
    span = lax.axis_index("blk")
    core = lax.axis_index("ulysses")
    row, col = span // 2, span % 2
    mine = span * 2 + core
    per_group = heads // groups
    width = per_group * DH
    parts = local_sem.shape[0]
    per_part = groups // parts
    half = groups // 2

    def block_of(r, c, u):
        return (r * 2 + c) * 2 + u

    targets = {
        UP: {"blk": span + 2, "ulysses": core},
        ACROSS: {"blk": row * 2 + 1 - col, "ulysses": core},
        CHIP: {"blk": span, "ulysses": 1 - core},
    }

    def remote(place, way, send_sem, recv_sem):
        return pltpu.make_async_remote_copy(
            src_ref=place,
            dst_ref=place,
            send_sem=send_sem,
            recv_sem=recv_sem,
            device_id=targets[way],
            device_id_type=MESH,
        )

    def piece(part, block):
        return kv_ref.at[pl.ds(part * per_part, per_part), block]

    def one(g, block):
        return kv_ref.at[pl.ds(g, 1), block]

    def up(part, k, block):
        return remote(piece(part, block), UP, up_send.at[0], up_recv.at[part, k])

    def across(part, k, block):
        return remote(piece(part, block), ACROSS, across_send.at[0], across_recv.at[part, k])

    def chip_own(part):
        return remote(piece(part, mine), CHIP, chip_send.at[0], pair_recv.at[0])

    def chip(part, k, block):
        return remote(piece(part, block), CHIP, chip_send.at[0], chip_recv.at[part, k - 1])

    def last_across(g, block):
        return remote(one(g, block), ACROSS, across_send.at[1], last_recv.at[g])

    def last_up(g, block):
        return remote(one(g, block), UP, up_send.at[1], last_recv.at[g])

    def last_chip(g, block):
        return remote(one(g, block), CHIP, chip_send.at[0], chip_last_recv.at[g % half])

    def local_copy(part, which, i):
        g = part * per_part + i
        return pltpu.make_async_copy(
            (k_hbm, v_hbm)[which].at[:, pl.ds(g * DH, DH)],
            kv_ref.at[g, mine, which],
            local_sem.at[part],
        )

    small = [
        pltpu.make_async_copy(src, dst, small_sem.at[i])
        for i, (src, dst) in enumerate(
            [(qs_hbm, qs_ref), (ks_hbm, ks_ref), (vert_hbm, vert_ref), (slash_hbm, slash_ref)]
        )
    ]
    to_scalars = pltpu.make_async_copy(table_ref, scalar_ref, small_sem.at[4])
    q_copy = pltpu.make_async_copy(q_hbm, q_ref, small_sem.at[5])
    barrier = pltpu.get_barrier_semaphore()
    below, above = row > 0, row < rows - 1

    @pl.when(above)
    def _():
        pl.semaphore_signal(
            barrier, inc=1, device_id={"blk": span + 2, "ulysses": core}, device_id_type=MESH
        )

    @pl.when(below)
    def _():
        pl.semaphore_signal(
            barrier, inc=1, device_id={"blk": span - 2, "ulysses": core}, device_id_type=MESH
        )

    for way in (ACROSS, CHIP):
        pl.semaphore_signal(barrier, inc=1, device_id=targets[way], device_id_type=MESH)
    for part in range(parts):
        for i in range(per_part):
            for which in (0, 1):
                local_copy(part, which, i).start()
    for copy in small:
        copy.start()
    pl.semaphore_wait(barrier, 2 + below.astype(jnp.int32) + above.astype(jnp.int32))

    for part in range(parts):
        pltpu.make_async_copy(piece(part, mine), piece(part, mine), local_sem.at[part]).wait()

        @pl.when(above)
        def _():
            up(part, 0, mine).start()

        @pl.when(below & (col == 0))
        def _():
            across(part, 0, mine).start()

        @pl.when(row == 0)
        def _():
            for i in range(per_part):
                last_across(part * per_part + i, mine).start()

        chip_own(part).start()

    q_copy.start()
    for copy in small:
        copy.wait()
    key_block = lax.broadcasted_iota(jnp.int32, (groups, 128), 1)
    slashes, verticals = slash_ref[...], vert_ref[...]
    hits = jnp.zeros((groups, 128), jnp.int32)
    for j in range(slashes.shape[1]):
        hits += jnp.where(key_block == mine - slashes[:, j : j + 1], 1, 0)
    for j in range(verticals.shape[1]):
        hits += jnp.where((key_block == verticals[:, j : j + 1]) & (key_block <= mine), 1, 0)
    table_ref[0] = jnp.where(hits > 0, 0.0, -BIG)
    table_ref[1, :, :blocks] = ks_ref[...].astype(jnp.float32) * LOG2E
    query_scales = qs_ref[...].astype(jnp.float32)
    table_ref[2, 0:1, :heads] = jnp.where(core == 0, query_scales[0:1], query_scales[1:2])
    to_scalars.start()

    token = lax.broadcasted_iota(jnp.int32, (BLOCK, BLOCK), 1)
    key_at = lax.broadcasted_iota(jnp.int32, (BLOCK, BLOCK), 0)
    later = jnp.where(key_at > token, 1.0, 0.0)
    eye = jnp.where(key_at == token, 1.0, 0.0).astype(jnp.bfloat16)

    def hidden(block, g):
        own = jnp.where(block == mine, -BIG, 0.0)
        return (scalar_ref[0, g, block] + later * own).astype(jnp.bfloat16)

    def dots(pairs, g, first):
        queries = jnp.concatenate(
            [
                jnp.concatenate(
                    [q_ref[:, pl.ds(pl.multiple_of(g * width + p * DH, DH), DH)], eye], axis=1
                )
                for p in range(per_group)
            ],
            axis=0,
        )
        scores = []
        for base in pairs:
            keys = kv_ref[g, pl.ds(base, 2), 0].reshape(2 * BLOCK, DH)
            masks = [
                hidden(base + i, g) if first
                else jnp.full((BLOCK, BLOCK), scalar_ref[0, g, base + i], jnp.float32).astype(jnp.bfloat16)
                for i in (0, 1)
            ]
            mask = jnp.concatenate(masks, axis=0)
            scores.append(
                lax.dot_general(
                    queries,
                    jnp.concatenate([keys, mask], axis=1),
                    (((1,), (1,)), ((), ())),
                    preferred_element_type=jnp.float32,
                )
            )
        return scores

    def unit(pairs, g, scores, first, last):
        scales = [scalar_ref[1, g, base + i] for base in pairs for i in (0, 1)]
        probs, alphas = [], []
        for p in range(per_group):
            here = slice(p * BLOCK, (p + 1) * BLOCK)
            q_scale = scalar_ref[2, 0, g * per_group + p]
            tiles = [
                scores[i // 2][here, (i % 2) * BLOCK : (i % 2 + 1) * BLOCK] * (q_scale * scales[i])
                for i in range(2 * len(pairs))
            ]
            top = functools.reduce(jnp.maximum, tiles)
            top = jnp.max(top, axis=1, keepdims=True)
            top = jnp.broadcast_to(top, (BLOCK, DH))
            if not first:
                old = m_ref[g, here, :]
                top = jnp.maximum(old, top)
                alpha = jnp.exp2(old - top)
                alphas.append(alpha)
            weights = [jnp.exp2(tile - top) for tile in tiles]
            total = functools.reduce(jnp.add, weights)
            if not first:
                total = l_ref[g, here, :] * alpha + total
            l_ref[g, here, :] = total
            if not last:
                m_ref[g, here, :] = top
            probs.append(jnp.concatenate([w.astype(jnp.bfloat16) for w in weights], axis=1))
        probs = jnp.concatenate(probs, axis=0)
        held = [kv_ref[g, pl.ds(base, 2), 1].reshape(2 * BLOCK, DH) for base in pairs]
        held = held[0] if len(held) == 1 else jnp.concatenate(held, axis=0)
        added = jnp.dot(probs, held, preferred_element_type=jnp.float32)
        for p in range(per_group):
            here = slice(p * BLOCK, (p + 1) * BLOCK)
            numer = added[here, :]
            if not first:
                numer = acc_ref[g, here, :] * alphas[p] + numer
            if last:
                total = jnp.sum(l_ref[g, here, :], axis=1, keepdims=True)
                o_ref[:, pl.ds(pl.multiple_of(g * width + p * DH, DH), DH)] = (
                    numer * (1.0 / total)
                ).astype(o_ref.dtype)
            else:
                acc_ref[g, here, :] = numer

    def units(pairs, kv_heads, first, last):
        scores = [dots(pairs, g, first) for g in kv_heads]
        for g, found in zip(kv_heads, scores):
            unit(pairs, g, found, first, last)

    q_copy.wait()
    to_scalars.wait()

    everything = kv_ref.at[:, mine]
    remote(everything, CHIP, chip_send.at[0], pair_recv.at[0]).wait_recv()

    @pl.loop(0, parts)
    def _(part):
        units([block_of(row, col, 0)], [part * per_part + i for i in range(per_part)], True, False)

    def pass_on(k, part):
        climbed = block_of(row - k, col, core)
        up(part, k - 1, climbed).wait_recv()

        chip(part, k, climbed).start()

        @pl.when(above)
        def _():
            up(part, k, climbed).start()

        @pl.when(k < row)
        def _():
            across(part, k, climbed).start()

        @pl.when(k == row)
        def _():
            for i in range(per_part):
                g = part * per_part + i

                @pl.when(g < half)
                def _():
                    last_across(g, climbed).start()

        crossed = block_of(row - k + 1, 1 - col, core)

        @pl.when((k > 1) | (col == 1))
        def _():
            across(part, k - 1, crossed).wait_recv()
            chip(part, k, crossed).start()

    crossed = block_of(0, 1 - col, core)

    def pass_last_on(g):
        last_across(g, crossed).wait_recv()

        last_chip(g, crossed).start()

        @pl.when(above & (g >= half))
        def _():
            last_up(g, crossed).start()

    turns = row * parts

    def climb(turn):
        k, part = 1 + turn // parts, turn % parts
        bases = [block_of(row - k, col, 0), block_of(row - k + 1, 1 - col, 0)]
        return k, part, bases

    def climb_arrived(turn):
        k, part, bases = climb(turn)
        both = kv_ref.at[pl.ds(part * per_part, per_part), pl.ds(bases[0], 2)]

        @pl.when((k > 1) | (col == 1))
        def _():
            remote(both, CHIP, chip_send.at[0], chip_recv.at[part, k - 1]).wait_recv()

        @pl.when((k == 1) & (col == 0))
        def _():
            chip(part, k, bases[0]).wait_recv()

    @pl.loop(0, turns)
    def _(turn):
        pass_on(1 + turn // parts, turn % parts)

        @pl.when(turn > 0)
        def _():
            climb_arrived(turn - 1)
            k, part, bases = climb(turn - 1)
            kv_heads = [part * per_part + i for i in range(per_part)]

            @pl.when((k > 1) | (col == 1))
            def _():
                units(bases, kv_heads, False, False)

            @pl.when((k == 1) & (col == 0))
            def _():
                units(bases[:1], kv_heads, False, False)

    def pass_both_on(step):
        pass_last_on(step + half)
        pass_last_on(step)

    @pl.when(below)
    def _():
        climb_arrived(turns - 1)
        k, part, bases = climb(turns - 1)

        pass_both_on(0)
        kv_heads = [part * per_part + i for i in range(per_part)]

        @pl.when((k > 1) | (col == 1))
        def _():
            units(bases, kv_heads, False, False)

        @pl.when((k == 1) & (col == 0))
        def _():
            units(bases[:1], kv_heads, False, False)

    @pl.when(row == 0)
    def _():
        pass_both_on(0)

    @pl.loop(0, half)
    def _(step):
        @pl.when(step < half - 1)
        def _():
            pass_both_on(step + 1)

        two = kv_ref.at[pl.ds(0, 2), crossed]
        remote(two, CHIP, chip_send.at[0], chip_last_recv.at[step]).wait_recv()
        units([block_of(0, 1 - col, 0)], [step, step + half], False, True)

    def sent(place, way, sem):
        remote(place, way, sem, pair_recv.at[0]).wait_send()

    lower = kv_ref.at[pl.ds(0, half), mine]

    @pl.when(below)
    def _():
        sent(lower, ACROSS, across_send.at[1])

    @pl.when(above)
    def _():
        sent(lower, UP, up_send.at[1])

    for r in range(rows):

        @pl.when(row == r)
        def _():
            if r == 0:
                sent(everything, ACROSS, across_send.at[1])
            else:
                @pl.when(col == 0)
                def _():
                    sent(kv_ref.at[:, pl.ds(0, r)], ACROSS, across_send.at[0])

                if r > 1:

                    @pl.when(col == 1)
                    def _():
                        sent(kv_ref.at[:, pl.ds(0, r - 1)], ACROSS, across_send.at[0])
            if r < rows - 1:
                sent(kv_ref.at[:, pl.ds(0, r + 1)], UP, up_send.at[0])
            for c in (0, 1):
                blocks_sent = 2 * r + 2 - (c == 0 and r > 0)

                @pl.when(col == c)
                def _():
                    sent(kv_ref.at[:, pl.ds(0, blocks_sent)], CHIP, chip_send.at[0])


def attend(mesh, query_int, key_int, values, query_scale, key_scale, verticals, slashes):
    spans = mesh.shape["blk"]
    tokens = query_int.shape[0]
    blocks = key_scale.shape[0]
    heads = query_int.shape[1] // DH
    groups = key_int.shape[1] // DH
    assert tokens == BLOCK and mesh.shape["ulysses"] == 2 and spans % 2 == 0
    assert blocks == spans * 2
    rows = spans // 2
    parts = 8
    assert groups % parts == 0 and groups % 2 == 0 and parts % 2 == 0 and rows > 1 and max(heads, blocks) <= 128
    per_group = heads // groups
    stack = (groups, per_group * BLOCK, DH)
    hbm = pl.BlockSpec(memory_space=pl.ANY)
    return pl.pallas_call(
        functools.partial(kernel, rows, heads, groups, blocks),
        out_shape=jax.ShapeDtypeStruct(query_int.shape, jnp.bfloat16),
        in_specs=[hbm] * 7,
        out_specs=pl.BlockSpec(memory_space=pltpu.VMEM),
        scratch_shapes=[
            pltpu.VMEM(query_int.shape, jnp.bfloat16),
            pltpu.VMEM((groups, blocks, 2, BLOCK, DH), jnp.bfloat16),
            pltpu.VMEM(stack, jnp.float32),
            pltpu.VMEM(stack, jnp.float32),
            pltpu.VMEM(stack, jnp.float32),
            pltpu.VMEM(query_scale.shape, query_scale.dtype),
            pltpu.VMEM(key_scale.shape[::-1], key_scale.dtype),
            pltpu.VMEM(verticals.shape, jnp.int32),
            pltpu.VMEM(slashes.shape, jnp.int32),
            pltpu.VMEM((3, groups, 128), jnp.float32),
            pltpu.SMEM((3, groups, 128), jnp.float32),
            pltpu.SemaphoreType.DMA((parts,)),
            pltpu.SemaphoreType.DMA((6,)),
            pltpu.SemaphoreType.DMA((2,)),
            pltpu.SemaphoreType.DMA((2,)),
            pltpu.SemaphoreType.DMA((1,)),
            pltpu.SemaphoreType.DMA((parts, rows - 1)),
            pltpu.SemaphoreType.DMA((parts, rows - 1)),
            pltpu.SemaphoreType.DMA((1,)),
            pltpu.SemaphoreType.DMA((parts, rows - 1)),
            pltpu.SemaphoreType.DMA((groups,)),
            pltpu.SemaphoreType.DMA((groups // 2,)),
        ],
        compiler_params=pltpu.CompilerParams(
            collective_id=0, has_side_effects=True, vmem_limit_bytes=(26 + blocks // 2) * 1024 * 1024
        ),
    )(*[pltpu.with_memory_space_constraint(x, pltpu.HBM) for x in (query_int, key_int, values, query_scale, key_scale.T, verticals, slashes)])


def solution(mesh):
    in_specs = (
        P(("group", "blk", "ulysses"), None),
        P(("group", "blk", "ulysses"), None),
        P(("group", "blk", "ulysses"), None),
        P(("group", "blk"), None),
        P("group", None),
        P("group", None),
        P("group", None),
    )
    out_specs = P(("group", "blk", "ulysses"), None)
    return jax.shard_map(
        functools.partial(attend, mesh),
        mesh=mesh,
        in_specs=in_specs,
        out_specs=out_specs,
        check_vma=False,
    )
```
